32 devices in a mesh: dp: 4 (over x, core), expert: 8 (over z, y).
Axes of the slice: x: 2, y: 2, z: 4, core: 2. Of those that a mesh axis runs over, the one named last changes fastest.
Arguments:
- x_online: bfloat16 [4096, 2048], P(('dp', 'expert')), may hold values from -6 to 6
- x_target: bfloat16 [4096, 2048], P(('dp', 'expert')), may hold values from -6 to 6
- routes: int32 [4096, 2], P(('dp', 'expert')), may hold values from 0 to 15, all different within a row; in each aligned block of 128 rows (0 to 127, 128 to 255, ...) at most 32 rows name the same one
- gate_probs: float32 [4096, 2], P(('dp', 'expert')), may hold values from 0.2 to 1
- expert_place: int32 [16], replicated, may hold values from 0 to 15, each once
- gate_online: bfloat16 [32, 2048, 256], P(('dp', 'expert')), may hold values from -0.125 to 0.125
- up_online: bfloat16 [32, 2048, 256], P(('dp', 'expert')), may hold values from -0.125 to 0.125
- down_online: bfloat16 [32, 256, 2048], P(('dp', 'expert')), may hold values from -0.25 to 0.25
- gate_target: bfloat16 [32, 2048, 256], P(('dp', 'expert')), may hold values from -0.125 to 0.125
- up_target: bfloat16 [32, 2048, 256], P(('dp', 'expert')), may hold values from -0.125 to 0.125
- down_target: bfloat16 [32, 256, 2048], P(('dp', 'expert')), may hold values from -0.25 to 0.25
Outputs:
- input_grad: bfloat16 [4096, 2048], P(('dp', 'expert'))
- grad_gate: bfloat16 [32, 2048, 256], P(('dp', 'expert'))
- grad_up: bfloat16 [32, 2048, 256], P(('dp', 'expert'))
- grad_down: bfloat16 [32, 256, 2048], P(('dp', 'expert'))
The draws below stay inside these ranges and needn't reach their ends.
Inputs may be any that keep to these rules, and one draw needn't show every extreme that they name: `routes`: each row names two different experts. Among the 128 rows of one device no expert is named more than 32 times, and in every draw some expert is named exactly 32 times by the rows of some device. `expert_place`: A permutation: each expert has a place of its own.
All inputs are finite; a program needn't handle non-finite values.
Results may differ from the reference program's by a relative error of at most 0.011.
Values may be sent and summed in bfloat16 or wider, within the bound.
A program may use at most 128 MiB of HBM per device.

```python
import math
import jax
import jax.numpy as jnp
import numpy as np
from jax import lax

D = 2048
FF = 512
TOK_DEV = 128
EXPERTS = 16
UNITS = 32
FF_HALF = 256
CAP = 32
TOKENS = 4096
N_DP = 4
N_EXPERT = 8


def levels(rng, shape, shards, least, high):
    factor_of, own = 1.0, jax.random.fold_in(rng, 6)
    for dim, shards_of in shards:
        draws = jnp.exp(jax.random.uniform(jax.random.fold_in(own, dim), (shards_of,), jnp.float32, least / len(shards), high / len(shards)))
        factor_of = factor_of * jnp.repeat(draws, shape[dim] // shards_of).reshape([-1 if axis == dim else 1 for axis in range(len(shape))])
    return factor_of


def assign_block(own_key, own, number, rows, amount, top, bound, skew):
    sequence = jax.random.permutation(own_key, amount)
    packed, usual = load_shares(amount, rows * top, bound, skew, True), load_shares(amount, rows * top, bound, skew, False)
    places = jnp.arange(amount)

    def named(sizes, turn):
        used = int((sizes > 0).sum())
        fixed = max(1, used // 4)
        passed = fixed + (places - fixed + turn * (used - fixed)) % max(1, amount - fixed)
        return jnp.zeros((amount,), jnp.int32).at[sequence[jnp.where(places < fixed, places, passed)]].set(jnp.asarray(sizes, jnp.int32))

    sizes = jnp.where(number % 4 == 0, named(packed, number // 4), named(usual, number - number // 4 - 1))
    mixed = jax.random.permutation(jax.random.fold_in(own, 3), amount)
    source_of, taker = mixed[0:amount // 2 * 2:2], mixed[1:amount // 2 * 2:2]
    slack = jnp.minimum(sizes[source_of] - 1, bound - sizes[taker]) // 2
    slack = jnp.where((source_of == sequence[0]) | (taker == sequence[0]) | (sizes[taker] == 0), 0, jnp.maximum(slack, 0))
    passed = jax.random.randint(jax.random.fold_in(own, 4), (amount // 2,), 0, 1 << 20) % (slack + 1)
    sizes = sizes.at[source_of].add(-passed).at[taker].add(passed)
    items = jnp.searchsorted(jnp.cumsum(sizes), jnp.arange(rows * top), side="right").astype(jnp.int32)
    listing = items.reshape(top, rows).T
    listing = listing[jax.random.permutation(jax.random.fold_in(own, 1), rows)]
    turn = jax.random.randint(jax.random.fold_in(own, 2), (rows, 1), 0, top)
    return jnp.take_along_axis(listing, (jnp.arange(top)[None, :] + turn) % top, axis=1)


def load_shares(count, total, limit, slope, full):
    loads = [(1 << 20) // math.isqrt(rank ** slope) + 1 for rank in range(1, count + 1)]
    largest = limit if full else min(limit, max(-(-total // count), total * loads[0] // sum(loads)))
    least = 1 if total - largest >= count - 1 else 0
    counts, surplus = [largest] + [least] * (count - 1), total - largest - least * (count - 1)
    while surplus > 0:
        candidates = [i for i in range(1, count) if counts[i] < largest] or [i for i in range(1, count) if counts[i] < limit]
        pool, budget = sum([loads[i] for i in candidates]), surplus
        for i in candidates:
            more = min(limit - counts[i], max(1, budget * loads[i] // pool), surplus)
            counts[i] = counts[i] + more
            surplus = surplus - more
    return np.array(counts)


def noise(rng, dims, spread, most, shards=(), kind=jnp.bfloat16):
    drawn = spread * jax.random.normal(rng, dims, jnp.float32)
    if shards:
        drawn = drawn * levels(rng, dims, shards, -0.22, 0.18)
    return jnp.clip(drawn, -most, most).astype(kind)


def setup_inputs(seed: int = 0) -> dict:
    splits = jax.random.split(jax.random.key(seed), 12)
    x_online = noise(splits[0], (TOKENS, D), 1.0, 6.0, ((0, 32),))
    x_target = noise(splits[1], (TOKENS, D), 1.0, 6.0, ((0, 32),))
    routes_keys = jax.random.split(jax.random.fold_in(splits[2], 1), TOKENS // TOK_DEV)
    routes_turns = jax.random.permutation(jax.random.fold_in(splits[2], 3), TOKENS // TOK_DEV)
    routes = jax.vmap(lambda own, number: assign_block(jax.random.fold_in(splits[2], 2), own, number, TOK_DEV, EXPERTS, 2, CAP, 2))(routes_keys, routes_turns).reshape((TOKENS, 2))
    gate_probs = jnp.clip(0.2 + 0.8 * jax.random.uniform(splits[3], (TOKENS, 2), jnp.float32) ** levels(splits[3], (TOKENS, 2), ((0, 32),), -0.2, 0.2), 0.2, 1.0)
    expert_place = jax.random.permutation(splits[4], EXPERTS).astype(jnp.int32)
    gate_online = noise(splits[5], (UNITS, D, FF_HALF), D ** -0.5, 0.125, ((0, 32),))
    up_online = noise(splits[6], (UNITS, D, FF_HALF), D ** -0.5, 0.125, ((0, 32),))
    down_online = noise(splits[7], (UNITS, FF_HALF, D), FF ** -0.5, 0.25, ((0, 32),))
    gate_target = noise(splits[8], (UNITS, D, FF_HALF), D ** -0.5, 0.125, ((0, 32),))
    up_target = noise(splits[9], (UNITS, D, FF_HALF), D ** -0.5, 0.125, ((0, 32),))
    down_target = noise(splits[10], (UNITS, FF_HALF, D), FF ** -0.5, 0.25, ((0, 32),))
    return dict(x_online=x_online, x_target=x_target, routes=routes, gate_probs=gate_probs, expert_place=expert_place, gate_online=gate_online, up_online=up_online, down_online=down_online, gate_target=gate_target, up_target=up_target, down_target=down_target)


contract_last = (((1,), (1,)), ((), ()))
contract_first = (((0,), (0,)), ((), ()))


def hidden_forward(inputs, w_gate, w_up):
    pre_gate = jnp.dot(inputs, w_gate, preferred_element_type=jnp.float32)
    pre_up = jnp.dot(inputs, w_up, preferred_element_type=jnp.float32)
    hidden = (jax.nn.silu(pre_gate) * pre_up).astype(jnp.bfloat16)
    return pre_gate, pre_up, hidden


def hidden_grads(cotangent, pre_gate, pre_up, w_down):
    d_hidden = lax.dot_general(cotangent, w_down, contract_last, preferred_element_type=jnp.float32)
    sigmoid_gate = jax.nn.sigmoid(pre_gate)
    d_gate = (d_hidden * pre_up * sigmoid_gate * (1.0 + pre_gate * (1.0 - sigmoid_gate))).astype(jnp.bfloat16)
    d_up = (d_hidden * jax.nn.silu(pre_gate)).astype(jnp.bfloat16)
    return d_gate, d_up


def input_rows(d_gate, d_up, w_gate, w_up):
    total = lax.dot_general(d_gate, w_gate, contract_last, preferred_element_type=jnp.float32)
    total = total + lax.dot_general(d_up, w_up, contract_last, preferred_element_type=jnp.float32)
    return total.astype(jnp.bfloat16)


def outer_sum(left, right):
    return lax.dot_general(left, right, contract_first, preferred_element_type=jnp.float32)


def whole_expert(w_gate, w_up, w_down, slot_index):
    pair_gate = lax.dynamic_slice_in_dim(w_gate, 2 * slot_index, 2, 0)
    pair_up = lax.dynamic_slice_in_dim(w_up, 2 * slot_index, 2, 0)
    pair_down = lax.dynamic_slice_in_dim(w_down, 2 * slot_index, 2, 0)
    gate_full = jnp.concatenate([pair_gate[0], pair_gate[1]], axis=1)
    up_full = jnp.concatenate([pair_up[0], pair_up[1]], axis=1)
    down_full = jnp.concatenate([pair_down[0], pair_down[1]], axis=0)
    return gate_full, up_full, down_full


def reference(x_online, x_target, routes, gate_probs, expert_place, gate_online, up_online, down_online, gate_target, up_target, down_target):
    blocks = N_DP * N_EXPERT
    per_expert = blocks * CAP
    assignments = 2 * TOKENS
    chosen = routes.reshape(blocks, 2 * TOK_DEV)
    expert_iota = jnp.arange(EXPERTS, dtype=jnp.int32)
    onehot = (chosen[:, :, None] == expert_iota[None, None, :]).astype(jnp.int32)
    before = jnp.cumsum(onehot, axis=1) - onehot
    position = jnp.sum(before * onehot, axis=2)
    slot_place = expert_place[chosen]
    block_index = jnp.arange(blocks, dtype=jnp.int32)[:, None]
    row_index = (slot_place * per_expert + block_index * CAP + position).reshape(-1).astype(jnp.int32)
    assignment = jnp.arange(assignments, dtype=jnp.int32)
    row_owner = jnp.full((EXPERTS * per_expert,), assignments, jnp.int32).at[row_index].set(assignment)
    filled = row_owner < assignments
    assign_of = jnp.minimum(row_owner, assignments - 1).astype(jnp.int32)
    token_of = (assign_of // 2).astype(jnp.int32)

    def slot_rows(source, index_table, slot_index):
        picked = lax.dynamic_slice_in_dim(index_table, slot_index * per_expert, per_expert)
        present = lax.dynamic_slice_in_dim(filled, slot_index * per_expert, per_expert)
        return jnp.where(present[:, None], source[picked], jnp.zeros((), source.dtype))

    def forward_slot(slot_index):
        inputs_online = slot_rows(x_online, token_of, slot_index)
        inputs_target = slot_rows(x_target, token_of, slot_index)
        gate_full, up_full, down_full = whole_expert(gate_online, up_online, down_online, slot_index)
        hidden = hidden_forward(inputs_online, gate_full, up_full)[2]
        out_online = jnp.dot(hidden, down_full, preferred_element_type=jnp.float32).astype(jnp.bfloat16)
        gate_full, up_full, down_full = whole_expert(gate_target, up_target, down_target, slot_index)
        hidden = hidden_forward(inputs_target, gate_full, up_full)[2]
        out_target = jnp.dot(hidden, down_full, preferred_element_type=jnp.float32).astype(jnp.bfloat16)
        return out_online, out_target

    slots = jnp.arange(EXPERTS, dtype=jnp.int32)
    outs_online, outs_target = lax.map(forward_slot, slots)
    y_online = jnp.sum(outs_online.reshape(-1, D)[row_index].reshape(TOKENS, 2, D).astype(jnp.float32) * gate_probs[:, :, None], axis=1)
    y_target = jnp.sum(outs_target.reshape(-1, D)[row_index].reshape(TOKENS, 2, D).astype(jnp.float32) * gate_probs[:, :, None], axis=1)
    cotangent = (gate_probs[:, :, None] * (y_online - y_target)[:, None, :]).astype(jnp.bfloat16).reshape(assignments, D)

    def backward_slot(slot_index):
        inputs_online = slot_rows(x_online, token_of, slot_index)
        cot_rows = slot_rows(cotangent, assign_of, slot_index)
        gate_full, up_full, down_full = whole_expert(gate_online, up_online, down_online, slot_index)
        pre_gate, pre_up, hidden = hidden_forward(inputs_online, gate_full, up_full)
        d_gate, d_up = hidden_grads(cot_rows, pre_gate, pre_up, down_full)
        d_rows = input_rows(d_gate, d_up, gate_full, up_full)
        g_gate = outer_sum(inputs_online, d_gate).astype(jnp.bfloat16)
        g_up = outer_sum(inputs_online, d_up).astype(jnp.bfloat16)
        g_down = outer_sum(hidden, cot_rows).astype(jnp.bfloat16)
        return d_rows, g_gate, g_up, g_down

    d_all, g_gate, g_up, g_down = lax.map(backward_slot, slots)
    input_grad = jnp.sum(d_all.reshape(-1, D)[row_index].reshape(TOKENS, 2, D).astype(jnp.float32), axis=1).astype(jnp.bfloat16)
    grad_gate = g_gate.reshape(EXPERTS, D, 2, FF_HALF).transpose(0, 2, 1, 3).reshape(UNITS, D, FF_HALF)
    grad_up = g_up.reshape(EXPERTS, D, 2, FF_HALF).transpose(0, 2, 1, 3).reshape(UNITS, D, FF_HALF)
    grad_down = g_down.reshape(UNITS, FF_HALF, D)
    return input_grad, grad_gate, grad_up, grad_down
```

```python
import functools

import jax
import jax.numpy as jnp
from jax import lax
from jax.experimental import pallas as pl
from jax.experimental.pallas import tpu as pltpu
from jax.sharding import PartitionSpec as P

contract_last = (((1,), (1,)), ((), ()))
contract_first = (((0,), (0,)), ((), ()))


def swapped(block, axis, bit):
    count = lax.axis_size(axis)
    route = []
    for low in range(count):
        high = low | 1 << bit
        if high != low and high < count:
            route += [(low, high), (high, low)]
    return lax.ppermute(block, axis, route)


def hidden_forward(inputs, w_gate, w_up):
    pre_gate = jnp.dot(inputs, w_gate, preferred_element_type=jnp.float32)
    pre_up = jnp.dot(inputs, w_up, preferred_element_type=jnp.float32)
    hidden = (jax.nn.silu(pre_gate) * pre_up).astype(jnp.bfloat16)
    return (pre_gate, pre_up, hidden)


def hidden_grads(cotangent, pre_gate, pre_up, w_down):
    d_hidden = lax.dot_general(cotangent, w_down, contract_last, preferred_element_type=jnp.float32)
    sigmoid_gate = jax.nn.sigmoid(pre_gate)
    d_gate = (d_hidden * pre_up * sigmoid_gate * (1.0 + pre_gate * (1.0 - sigmoid_gate))).astype(
        jnp.bfloat16
    )
    d_up = (d_hidden * jax.nn.silu(pre_gate)).astype(jnp.bfloat16)
    return (d_gate, d_up)


def input_rows(d_gate, d_up, w_gate, w_up):
    total = lax.dot_general(d_gate, w_gate, contract_last, preferred_element_type=jnp.float32)
    total = total + lax.dot_general(d_up, w_up, contract_last, preferred_element_type=jnp.float32)
    return total.astype(jnp.bfloat16)


def outer_sum(left, right):
    return lax.dot_general(left, right, contract_first, preferred_element_type=jnp.float32)


def earlier_same(chosen):
    turn = jnp.arange(chosen.shape[0], dtype=jnp.int32)
    alike = (chosen[:, None] == chosen[None, :]) & (turn[None, :] < turn[:, None])
    return jnp.sum(alike.astype(jnp.int32), axis=1)


def shards_plain(
    x_online,
    x_target,
    routes,
    gate_probs,
    expert_place,
    gate_online,
    up_online,
    down_online,
    gate_target,
    up_target,
    down_target,
):
    tok_rows, model_width = x_online.shape
    dp_count = lax.axis_size("dp")
    expert_count = lax.axis_size("expert")
    unit_count = dp_count * expert_count
    experts = expert_place.shape[0]
    capacity = 2 * ((2 * tok_rows + experts - 1) // experts)
    half_cap = capacity // 2
    half_width = gate_online.shape[2]
    chosen = routes.reshape(-1)
    onehot = (chosen[:, None] == jnp.arange(experts, dtype=jnp.int32)[None, :]).astype(jnp.int32)
    position = earlier_same(chosen)
    slot_place = jnp.sum(onehot * expert_place[None, :], axis=1)
    flat_slot = (2 * slot_place + position // half_cap) * half_cap + position % half_cap
    owner_token = jnp.arange(2 * tok_rows, dtype=jnp.int32) // 2

    def to_units(source):
        blank_rows = jnp.zeros((unit_count * half_cap, model_width), source.dtype)
        return (
            blank_rows.at[flat_slot]
            .set(source)
            .reshape(dp_count, expert_count, half_cap, model_width)
        )

    def from_units(block):
        picked = block.reshape(unit_count * half_cap, model_width)[flat_slot]
        return picked.astype(jnp.float32).reshape(tok_rows, 2, model_width)

    partner = swapped(
        (gate_online, up_online, down_online, gate_target, up_target, down_target), "expert", 0
    )
    gate_full = jnp.concatenate([gate_online[0], partner[0][0]], axis=1)
    up_full = jnp.concatenate([up_online[0], partner[1][0]], axis=1)
    down_full = jnp.concatenate([down_online[0], partner[2][0]], axis=0)
    gate_tfull = jnp.concatenate([gate_target[0], partner[3][0]], axis=1)
    up_tfull = jnp.concatenate([up_target[0], partner[4][0]], axis=1)
    down_tfull = jnp.concatenate([down_target[0], partner[5][0]], axis=0)
    recv_online, recv_target = (
        lax.all_to_all(
            lax.all_to_all(
                to_units(x_online[owner_token]), "dp", split_axis=0, concat_axis=0, tiled=True
            ),
            "expert",
            split_axis=1,
            concat_axis=1,
            tiled=True,
        ),
        lax.all_to_all(
            lax.all_to_all(
                to_units(x_target[owner_token]), "dp", split_axis=0, concat_axis=0, tiled=True
            ),
            "expert",
            split_axis=1,
            concat_axis=1,
            tiled=True,
        ),
    )
    unit_shape = recv_online.shape
    inputs_online = recv_online.reshape(-1, model_width)
    inputs_target = recv_target.reshape(-1, model_width)
    pre_gate, pre_up, hidden = hidden_forward(inputs_online, gate_full, up_full)
    out_online = jnp.dot(hidden, down_full, preferred_element_type=jnp.float32).astype(jnp.bfloat16)
    hidden_target = hidden_forward(inputs_target, gate_tfull, up_tfull)[2]
    out_target = jnp.dot(hidden_target, down_tfull, preferred_element_type=jnp.float32).astype(
        jnp.bfloat16
    )
    back_online, back_target = (
        lax.all_to_all(
            lax.all_to_all(
                out_online.reshape(unit_shape), "dp", split_axis=0, concat_axis=0, tiled=True
            ),
            "expert",
            split_axis=1,
            concat_axis=1,
            tiled=True,
        ),
        lax.all_to_all(
            lax.all_to_all(
                out_target.reshape(unit_shape), "dp", split_axis=0, concat_axis=0, tiled=True
            ),
            "expert",
            split_axis=1,
            concat_axis=1,
            tiled=True,
        ),
    )
    y_online = jnp.sum(from_units(back_online) * gate_probs[:, :, None], axis=1)
    y_target = jnp.sum(from_units(back_target) * gate_probs[:, :, None], axis=1)
    cotangent = (
        (gate_probs[:, :, None] * (y_online - y_target)[:, None, :])
        .astype(jnp.bfloat16)
        .reshape(2 * tok_rows, model_width)
    )
    cot_recv = lax.all_to_all(
        lax.all_to_all(to_units(cotangent), "dp", split_axis=0, concat_axis=0, tiled=True),
        "expert",
        split_axis=1,
        concat_axis=1,
        tiled=True,
    )
    cot_rows = cot_recv.reshape(-1, model_width)
    d_gate, d_up = hidden_grads(cot_rows, pre_gate, pre_up, down_full)
    d_rows = input_rows(d_gate, d_up, gate_full, up_full)
    back_grads = lax.all_to_all(
        lax.all_to_all(d_rows.reshape(unit_shape), "dp", split_axis=0, concat_axis=0, tiled=True),
        "expert",
        split_axis=1,
        concat_axis=1,
        tiled=True,
    )
    input_grad = jnp.sum(from_units(back_grads), axis=1).astype(jnp.bfloat16)
    g_gate = outer_sum(inputs_online, d_gate)
    g_up = outer_sum(inputs_online, d_up)
    g_down = outer_sum(hidden, cot_rows)
    sent = (
        swapped(g_gate[:, half_width:].astype(jnp.bfloat16), "expert", 0).astype(jnp.float32),
        swapped(g_up[:, half_width:].astype(jnp.bfloat16), "expert", 0).astype(jnp.float32),
        swapped(g_down[half_width:].astype(jnp.bfloat16), "expert", 0).astype(jnp.float32),
    )
    grad_gate = g_gate[:, :half_width] + sent[0]
    grad_up = g_up[:, :half_width] + sent[1]
    grad_down = g_down[:half_width] + sent[2]
    return (
        input_grad,
        grad_gate.astype(jnp.bfloat16)[None],
        grad_up.astype(jnp.bfloat16)[None],
        grad_down.astype(jnp.bfloat16)[None],
    )


MESH = pl.DeviceIdType.MESH
F32 = jnp.float32
BF16 = jnp.bfloat16


def dot(left, right, dims=(((1,), (0,)), ((), ()))):
    return lax.dot_general(left, right, dims, preferred_element_type=F32)


def step_kernel(
    slots,
    n_ex,
    cap,
    routes_ref,
    probs_ref,
    place_ref,
    xo_ref,
    xt_ref,
    w0_ref,
    w1_ref,
    w2_ref,
    w3_ref,
    w4_ref,
    w5_ref,
    ig_ref,
    gg_ref,
    gu_ref,
    gd_ref,
    wg,
    wu,
    wd,
    sx,
    rx,
    pd,
    pr,
    ret,
    rc,
    pre_g,
    pre_u,
    hid,
    dgu,
    w_sem,
    send_sem,
    recv_sem,
    fsend_sem,
    frecv_sem,
    ysend_sem,
    yrecv_sem,
    bsend_sem,
    brecv_sem,
):
    tok, width = xo_ref.shape
    rows = slots * cap
    half = wg.shape[2]
    tile = 512
    dp, ex = lax.axis_index("dp"), lax.axis_index("expert")
    side = lax.rem(ex, 2)
    me = lax.div(dp * n_ex + ex, 2)
    partner = (dp, ex + 1 - 2 * side)

    planes = n_ex // 2
    group = slots // planes
    near, window = slots // 2, 5

    def other(i):
        mask = lax.rem(i, group) * planes + lax.div(i, group)
        slot, power = 0, 1
        while power < slots:
            bit = lax.rem(lax.rem(lax.div(me, power), 2) + lax.rem(lax.div(mask, power), 2), 2)
            slot, power = slot + bit * power, 2 * power
        return slot

    def peer(slot):
        unit = 2 * slot + side
        return (lax.div(unit, n_ex), lax.rem(unit, n_ex))

    def chunk(index):
        return pl.ds(pl.multiple_of(index * cap, cap), cap)

    barrier = pltpu.get_barrier_semaphore()

    def greet(o, carry):
        pl.semaphore_signal(
            barrier, inc=1, device_id=peer(other(o)), device_id_type=MESH
        )
        return carry

    lax.fori_loop(1, slots, greet, 0)
    pl.semaphore_signal(barrier, inc=1, device_id=partner, device_id_type=MESH)

    weight_copies = [
        pltpu.make_async_copy(source, target, w_sem.at[i])
        for i, (source, target) in enumerate(
            [
                (w0_ref, wg.at[0]),
                (w1_ref, wu.at[0]),
                (w2_ref, wd.at[0]),
                (w3_ref, wg.at[1]),
                (w4_ref, wu.at[1]),
                (w5_ref, wd.at[1]),
            ]
        )
    ]
    for copy in weight_copies:
        copy.start()

    def one_hot(compare):
        return jnp.where(compare, 1.0, 0.0).astype(BF16)

    down, across = [lax.broadcasted_iota(jnp.int32, (tok, tok), d) for d in range(2)]

    def stand(line):
        size = line.shape[1]
        here = [lax.broadcasted_iota(jnp.int32, (size, size), d) for d in range(2)]
        return jnp.sum(jnp.where(here[0] == here[1], line, 0.0), axis=1, keepdims=True)

    def count(mask, axis):
        return jnp.sum(jnp.where(mask, 1.0, 0.0), axis=axis, keepdims=True)

    line = [routes_ref[k : k + 1, :].astype(F32) for k in range(2)]
    tall = [stand(line[k]) for k in range(2)]
    place = place_ref[...].astype(F32)
    place_tall = stand(place)
    ids_line = lax.broadcasted_iota(jnp.int32, (tok, slots), 1).astype(F32)
    ids_tall = lax.broadcasted_iota(jnp.int32, (slots, tok), 0).astype(F32)
    flat_line, flat_tall = [], []
    for k in range(2):
        alike = (line[k] == tall[0]) | (line[k] == tall[1])
        slot = jnp.sum(jnp.where(ids_tall == line[k], place_tall, 0.0), axis=0, keepdims=True)
        flat_line.append((slot * cap + count(alike & (down < across), 0)).astype(jnp.int32))
        alike = (tall[k] == line[0]) | (tall[k] == line[1])
        slot = jnp.sum(jnp.where(ids_line == tall[k], place, 0.0), axis=1, keepdims=True)
        flat_tall.append((slot * cap + count(alike & (across < down), 1)).astype(jnp.int32))

    row_iota = lax.broadcasted_iota(jnp.int32, (rows, tok), 0)
    put = [one_hot(row_iota == flat_line[k]) for k in range(2)]
    put_any = one_hot((row_iota == flat_line[0]) | (row_iota == flat_line[1]))
    col_iota = lax.broadcasted_iota(jnp.int32, (tok, rows), 1)
    take = [one_hot(col_iota == flat_tall[k]) for k in range(2)]
    take_any = one_hot((col_iota == flat_tall[0]) | (col_iota == flat_tall[1]))

    def columns(body, low=0, high=width):
        def step(i, carry):
            body(pl.ds(pl.multiple_of(i * tile, tile), tile))
            return carry

        lax.fori_loop(low // tile, high // tile, step, 0)

    middle = width // 2
    span = [(0, middle), (middle, width)]

    def part_of(net):
        return pl.ds(*(((net % 2) * middle, middle) if net >= 2 else (0, width)))

    def each(low, body, high=slots):
        def step(o, carry):
            body(o)
            return carry

        lax.fori_loop(low, high, step, 0)

    def each_down(low, body):
        each(0, lambda o: body(slots - 1 - o), slots - low)

    def out_copy(net, dst, o):
        to = other(o)
        return pltpu.make_async_remote_copy(
            src_ref=sx.at[min(net, 2), chunk(to), part_of(net)],
            dst_ref=dst.at[0, chunk(o), part_of(net)],
            send_sem=send_sem.at[net, o],
            recv_sem=recv_sem.at[net, o],
            device_id=peer(to),
            device_id_type=MESH,
        )

    def fwd_copy(net, dst, o):
        return pltpu.make_async_remote_copy(
            src_ref=dst.at[0, chunk(o), part_of(net)],
            dst_ref=dst.at[1, chunk(o), part_of(net)],
            send_sem=fsend_sem.at[net, o],
            recv_sem=frecv_sem.at[net, o],
            device_id=partner,
            device_id_type=MESH,
        )

    def start_near(net, dst):
        each(1, lambda o: out_copy(net, dst, o).start(), near)
        dst[0, 0:cap, part_of(net)] = sx[min(net, 2), chunk(me), part_of(net)]
        fwd_copy(net, dst, 0).start()

    def start_far(net, dst):
        each(near, lambda o: out_copy(net, dst, o).start(), near + window)

    def relay(net, dst, then=None):
        def pass_on(o):
            out_copy(net, dst, o).wait_recv()
            fwd_copy(net, dst, o).start()

        def far(o):
            pass_on(o)
            out_copy(net, dst, o).wait_send()
            out_copy(net, dst, o + window).start()

        def last(o):
            pass_on(o)
            out_copy(net, dst, o).wait_send()
            if then is not None:
                out_copy(*then, o - (slots - window - near)).start()

        each(1, pass_on, near)
        if then is not None:
            start_near(*then)
        each(near, far, slots - window)
        each(slots - window, last)

    def arrived(net, dst):
        each(0, lambda o: fwd_copy(net, dst, o).wait_recv())

    def scatter_end(net, dst):
        each(0, lambda o: fwd_copy(net, dst, o).wait_send())
        each(1, lambda o: out_copy(net, dst, o).wait_send(), near)

    def half_of(turn):
        return pl.ds((turn % 2) * middle, middle)

    def pair_copy(turn, o):
        return pltpu.make_async_remote_copy(
            src_ref=pd.at[1, chunk(o), half_of(turn)],
            dst_ref=pr.at[turn // 2, chunk(o), half_of(turn)],
            send_sem=ysend_sem.at[turn, o],
            recv_sem=yrecv_sem.at[turn, o],
            device_id=partner,
            device_id_type=MESH,
        )

    def back_copy(turn, o):
        return pltpu.make_async_remote_copy(
            src_ref=pd.at[0, chunk(o), half_of(turn)],
            dst_ref=ret.at[turn // 2, chunk(me), half_of(turn)],
            send_sem=bsend_sem.at[turn, o],
            recv_sem=brecv_sem.at[turn, o],
            device_id=peer(other(o)),
            device_id_type=MESH,
        )

    def add_part(turn, o):
        pair_copy(turn, o).wait_recv()
        cols = half_of(turn)
        total = pd[0, chunk(o), cols].astype(F32) + pr[turn // 2, chunk(o), cols].astype(F32)
        return total.astype(BF16)

    def give_back(turn):
        def body(o):
            pd[0, chunk(o), half_of(turn)] = add_part(turn, o)
            back_copy(turn, o).start()

        each_down(1, body)
        ret[turn // 2, chunk(me), half_of(turn)] = add_part(turn, 0)

    def back_sent(turn):
        each(0, lambda o: pair_copy(turn, o).wait_send())
        each(1, lambda o: back_copy(turn, o).wait_send())

    def back_came(turn):
        each(1, lambda o: back_copy(turn, o).wait_recv())

    def place_online(cols):
        sx[0, :, cols] = dot(put_any, xo_ref[:, cols]).astype(BF16)

    def place_target(cols):
        sx[1, :, cols] = dot(put_any, xt_ref[:, cols]).astype(BF16)

    columns(place_online)
    pl.semaphore_wait(barrier, slots)
    start_far(0, rx.at[0])
    start_near(0, rx.at[0])
    columns(place_target)
    for copy in weight_copies:
        copy.wait()
    relay(0, rx.at[0], (1, rx.at[1]))
    relay(1, rx.at[1])

    def forward(net, part):
        gate = dot(rx[net, part], wg[net])
        up = dot(rx[net, part], wu[net])
        hid[net, part] = (gate * jax.nn.sigmoid(gate) * up).astype(BF16)
        if net == 0:
            pre_g[part] = gate
            pre_u[part] = up

    forward(0, 0)
    arrived(0, rx.at[0])
    forward(0, 1)
    forward(1, 0)
    arrived(1, rx.at[1])
    forward(1, 1)

    for side_part in (1, 0):

        def outputs(cols, part=side_part):
            diff = dot(hid[0, part], wd[0, :, cols]) - dot(hid[1, part], wd[1, :, cols])
            pd[part, :, cols] = diff.astype(BF16)

        for turn in (0, 1):
            columns(outputs, *span[turn])
            if side_part == 1:
                each_down(0, lambda o, turn=turn: pair_copy(turn, o).start())
    give_back(0)
    give_back(1)

    p0, p1 = [stand(probs_ref[k : k + 1, :]) for k in range(2)]

    def cotangents(cols):
        back = ret[0, :, cols]
        diff = p0 * dot(take[0], back) + p1 * dot(take[1], back)
        cot0, cot1 = (p0 * diff).astype(BF16), (p1 * diff).astype(BF16)
        sx[2, :, cols] = (dot(put[0], cot0) + dot(put[1], cot1)).astype(BF16)

    back_came(0)
    columns(cotangents, *span[0])
    start_far(2, rc)
    start_near(2, rc)
    back_came(1)
    columns(cotangents, *span[1])
    relay(2, rc, (3, rc))
    relay(3, rc)
    scatter_end(0, rx.at[0])
    scatter_end(1, rx.at[1])
    back_sent(0)
    back_sent(1)

    def hidden_back(part):
        d_hidden = dot(rc[part], wd[0], contract_last)
        gate, up = pre_g[part], pre_u[part]
        sig = jax.nn.sigmoid(gate)
        dgu[0, part] = (d_hidden * up * sig * (1.0 + gate * (1.0 - sig))).astype(BF16)
        dgu[1, part] = (d_hidden * (gate * sig)).astype(BF16)

    hidden_back(0)
    arrived(2, rc)
    arrived(3, rc)
    hidden_back(1)
    for side_part in (1, 0):

        def row_grads(cols, part=side_part):
            total = dot(dgu[0, part], wg[0, cols, :], contract_last)
            total = total + dot(dgu[1, part], wu[0, cols, :], contract_last)
            pd[part, :, cols] = total.astype(BF16)

        for turn in (2, 3):
            columns(row_grads, *span[turn - 2])
            if side_part == 1:
                each_down(0, lambda o, turn=turn: pair_copy(turn, o).start())
    give_back(2)
    give_back(3)

    def weight_grads(cols):
        for index, target in ((0, gg_ref), (1, gu_ref)):
            total = dot(rx[0, 0, :, cols], dgu[index, 0], contract_first)
            total = total + dot(rx[0, 1, :, cols], dgu[index, 1], contract_first)
            target[cols, :] = total.astype(BF16)
        total = dot(hid[0, 0], rc[0, :, cols], contract_first)
        total = total + dot(hid[0, 1], rc[1, :, cols], contract_first)
        gd_ref[:, cols] = total.astype(BF16)

    columns(weight_grads)
    scatter_end(2, rc)
    scatter_end(3, rc)
    back_came(2)

    def inputs_grad(cols):
        ig_ref[:, cols] = dot(take_any, ret[1, :, cols]).astype(BF16)

    columns(inputs_grad, *span[0])
    back_came(3)
    columns(inputs_grad, *span[1])
    back_sent(2)
    back_sent(3)


def shards(
    x_online,
    x_target,
    routes,
    gate_probs,
    expert_place,
    gate_online,
    up_online,
    down_online,
    gate_target,
    up_target,
    down_target,
):
    tok, width = x_online.shape
    slots = expert_place.shape[0]
    n_ex = lax.axis_size("expert")
    cap = 2 * ((2 * tok + slots - 1) // slots)
    rows = slots * cap
    half = gate_online.shape[2]
    paired = 2 * slots == lax.axis_size("dp") * n_ex and n_ex % 2 == 0
    halving = slots & (slots - 1) == 0 and n_ex & (n_ex - 1) == 0
    if cap % 16 or width % 1024 or slots < 16 or not (paired and halving):
        return shards_plain(
            x_online,
            x_target,
            routes,
            gate_probs,
            expert_place,
            gate_online,
            up_online,
            down_online,
            gate_target,
            up_target,
            down_target,
        )
    vmem = pl.BlockSpec(memory_space=pltpu.VMEM)
    hbm = pl.BlockSpec(memory_space=pl.ANY)
    dma = pltpu.SemaphoreType.DMA
    outs = pl.pallas_call(
        functools.partial(step_kernel, slots, n_ex, cap),
        out_shape=(
            jax.ShapeDtypeStruct((tok, width), BF16),
            jax.ShapeDtypeStruct((width, half), BF16),
            jax.ShapeDtypeStruct((width, half), BF16),
            jax.ShapeDtypeStruct((half, width), BF16),
        ),
        in_specs=[vmem] * 5 + [hbm] * 6,
        out_specs=(vmem,) * 4,
        scratch_shapes=[
            pltpu.VMEM((2, width, half), BF16),
            pltpu.VMEM((2, width, half), BF16),
            pltpu.VMEM((2, half, width), BF16),
            pltpu.VMEM((3, rows, width), BF16),
            pltpu.VMEM((2, 2, rows, width), BF16),
            pltpu.VMEM((2, rows, width), BF16),
            pltpu.VMEM((2, rows, width), BF16),
            pltpu.VMEM((2, rows, width), BF16),
            pltpu.VMEM((2, rows, width), BF16),
            pltpu.VMEM((2, rows, half), F32),
            pltpu.VMEM((2, rows, half), F32),
            pltpu.VMEM((2, 2, rows, half), BF16),
            pltpu.VMEM((2, 2, rows, half), BF16),
            dma((6,)),
            dma((4, slots)),
            dma((4, slots)),
            dma((4, slots)),
            dma((4, slots)),
            dma((4, slots)),
            dma((4, slots)),
            dma((4, slots)),
            dma((4, slots)),
        ],
        compiler_params=pltpu.CompilerParams(
            collective_id=0, has_side_effects=True, vmem_limit_bytes=60 * 2**20
        ),
    )(
        routes.T,
        gate_probs.T,
        expert_place[None],
        x_online,
        x_target,
        gate_online[0],
        up_online[0],
        down_online[0],
        gate_target[0],
        up_target[0],
        down_target[0],
    )
    return (outs[0], outs[1][None], outs[2][None], outs[3][None])


def solution(mesh):
    in_specs = (
        P(("dp", "expert"), None),
        P(("dp", "expert"), None),
        P(("dp", "expert"), None),
        P(("dp", "expert"), None),
        P(),
        P(("dp", "expert"), None, None),
        P(("dp", "expert"), None, None),
        P(("dp", "expert"), None, None),
        P(("dp", "expert"), None, None),
        P(("dp", "expert"), None, None),
        P(("dp", "expert"), None, None),
    )
    out_specs = (
        P(("dp", "expert"), None),
        P(("dp", "expert"), None, None),
        P(("dp", "expert"), None, None),
        P(("dp", "expert"), None, None),
    )
    return jax.shard_map(shards, mesh=mesh, in_specs=in_specs, out_specs=out_specs, check_vma=False)
```

```python
import functools

import jax
import jax.numpy as jnp
from jax import lax
from jax.experimental import pallas as pl
from jax.experimental.pallas import tpu as pltpu
from jax.sharding import PartitionSpec as P

contract_last = (((1,), (1,)), ((), ()))
contract_first = (((0,), (0,)), ((), ()))


def swapped(block, axis, bit):
    count = lax.axis_size(axis)
    route = []
    for low in range(count):
        high = low | 1 << bit
        if high != low and high < count:
            route += [(low, high), (high, low)]
    return lax.ppermute(block, axis, route)


def hidden_forward(inputs, w_gate, w_up):
    pre_gate = jnp.dot(inputs, w_gate, preferred_element_type=jnp.float32)
    pre_up = jnp.dot(inputs, w_up, preferred_element_type=jnp.float32)
    hidden = (jax.nn.silu(pre_gate) * pre_up).astype(jnp.bfloat16)
    return (pre_gate, pre_up, hidden)


def hidden_grads(cotangent, pre_gate, pre_up, w_down):
    d_hidden = lax.dot_general(cotangent, w_down, contract_last, preferred_element_type=jnp.float32)
    sigmoid_gate = jax.nn.sigmoid(pre_gate)
    d_gate = (d_hidden * pre_up * sigmoid_gate * (1.0 + pre_gate * (1.0 - sigmoid_gate))).astype(
        jnp.bfloat16
    )
    d_up = (d_hidden * jax.nn.silu(pre_gate)).astype(jnp.bfloat16)
    return (d_gate, d_up)


def input_rows(d_gate, d_up, w_gate, w_up):
    total = lax.dot_general(d_gate, w_gate, contract_last, preferred_element_type=jnp.float32)
    total = total + lax.dot_general(d_up, w_up, contract_last, preferred_element_type=jnp.float32)
    return total.astype(jnp.bfloat16)


def outer_sum(left, right):
    return lax.dot_general(left, right, contract_first, preferred_element_type=jnp.float32)


def earlier_same(chosen):
    turn = jnp.arange(chosen.shape[0], dtype=jnp.int32)
    alike = (chosen[:, None] == chosen[None, :]) & (turn[None, :] < turn[:, None])
    return jnp.sum(alike.astype(jnp.int32), axis=1)


def shards_plain(
    x_online,
    x_target,
    routes,
    gate_probs,
    expert_place,
    gate_online,
    up_online,
    down_online,
    gate_target,
    up_target,
    down_target,
):
    tok_rows, model_width = x_online.shape
    dp_count = lax.axis_size("dp")
    expert_count = lax.axis_size("expert")
    unit_count = dp_count * expert_count
    experts = expert_place.shape[0]
    capacity = 2 * ((2 * tok_rows + experts - 1) // experts)
    half_cap = capacity // 2
    half_width = gate_online.shape[2]
    chosen = routes.reshape(-1)
    onehot = (chosen[:, None] == jnp.arange(experts, dtype=jnp.int32)[None, :]).astype(jnp.int32)
    position = earlier_same(chosen)
    slot_place = jnp.sum(onehot * expert_place[None, :], axis=1)
    flat_slot = (2 * slot_place + position // half_cap) * half_cap + position % half_cap
    owner_token = jnp.arange(2 * tok_rows, dtype=jnp.int32) // 2

    def to_units(source):
        blank_rows = jnp.zeros((unit_count * half_cap, model_width), source.dtype)
        return (
            blank_rows.at[flat_slot]
            .set(source)
            .reshape(dp_count, expert_count, half_cap, model_width)
        )

    def from_units(block):
        picked = block.reshape(unit_count * half_cap, model_width)[flat_slot]
        return picked.astype(jnp.float32).reshape(tok_rows, 2, model_width)

    partner = swapped(
        (gate_online, up_online, down_online, gate_target, up_target, down_target), "expert", 0
    )
    gate_full = jnp.concatenate([gate_online[0], partner[0][0]], axis=1)
    up_full = jnp.concatenate([up_online[0], partner[1][0]], axis=1)
    down_full = jnp.concatenate([down_online[0], partner[2][0]], axis=0)
    gate_tfull = jnp.concatenate([gate_target[0], partner[3][0]], axis=1)
    up_tfull = jnp.concatenate([up_target[0], partner[4][0]], axis=1)
    down_tfull = jnp.concatenate([down_target[0], partner[5][0]], axis=0)
    recv_online, recv_target = (
        lax.all_to_all(
            lax.all_to_all(
                to_units(x_online[owner_token]), "dp", split_axis=0, concat_axis=0, tiled=True
            ),
            "expert",
            split_axis=1,
            concat_axis=1,
            tiled=True,
        ),
        lax.all_to_all(
            lax.all_to_all(
                to_units(x_target[owner_token]), "dp", split_axis=0, concat_axis=0, tiled=True
            ),
            "expert",
            split_axis=1,
            concat_axis=1,
            tiled=True,
        ),
    )
    unit_shape = recv_online.shape
    inputs_online = recv_online.reshape(-1, model_width)
    inputs_target = recv_target.reshape(-1, model_width)
    pre_gate, pre_up, hidden = hidden_forward(inputs_online, gate_full, up_full)
    out_online = jnp.dot(hidden, down_full, preferred_element_type=jnp.float32).astype(jnp.bfloat16)
    hidden_target = hidden_forward(inputs_target, gate_tfull, up_tfull)[2]
    out_target = jnp.dot(hidden_target, down_tfull, preferred_element_type=jnp.float32).astype(
        jnp.bfloat16
    )
    back_online, back_target = (
        lax.all_to_all(
            lax.all_to_all(
                out_online.reshape(unit_shape), "dp", split_axis=0, concat_axis=0, tiled=True
            ),
            "expert",
            split_axis=1,
            concat_axis=1,
            tiled=True,
        ),
        lax.all_to_all(
            lax.all_to_all(
                out_target.reshape(unit_shape), "dp", split_axis=0, concat_axis=0, tiled=True
            ),
            "expert",
            split_axis=1,
            concat_axis=1,
            tiled=True,
        ),
    )
    y_online = jnp.sum(from_units(back_online) * gate_probs[:, :, None], axis=1)
    y_target = jnp.sum(from_units(back_target) * gate_probs[:, :, None], axis=1)
    cotangent = (
        (gate_probs[:, :, None] * (y_online - y_target)[:, None, :])
        .astype(jnp.bfloat16)
        .reshape(2 * tok_rows, model_width)
    )
    cot_recv = lax.all_to_all(
        lax.all_to_all(to_units(cotangent), "dp", split_axis=0, concat_axis=0, tiled=True),
        "expert",
        split_axis=1,
        concat_axis=1,
        tiled=True,
    )
    cot_rows = cot_recv.reshape(-1, model_width)
    d_gate, d_up = hidden_grads(cot_rows, pre_gate, pre_up, down_full)
    d_rows = input_rows(d_gate, d_up, gate_full, up_full)
    back_grads = lax.all_to_all(
        lax.all_to_all(d_rows.reshape(unit_shape), "dp", split_axis=0, concat_axis=0, tiled=True),
        "expert",
        split_axis=1,
        concat_axis=1,
        tiled=True,
    )
    input_grad = jnp.sum(from_units(back_grads), axis=1).astype(jnp.bfloat16)
    g_gate = outer_sum(inputs_online, d_gate)
    g_up = outer_sum(inputs_online, d_up)
    g_down = outer_sum(hidden, cot_rows)
    sent = (
        swapped(g_gate[:, half_width:].astype(jnp.bfloat16), "expert", 0).astype(jnp.float32),
        swapped(g_up[:, half_width:].astype(jnp.bfloat16), "expert", 0).astype(jnp.float32),
        swapped(g_down[half_width:].astype(jnp.bfloat16), "expert", 0).astype(jnp.float32),
    )
    grad_gate = g_gate[:, :half_width] + sent[0]
    grad_up = g_up[:, :half_width] + sent[1]
    grad_down = g_down[:half_width] + sent[2]
    return (
        input_grad,
        grad_gate.astype(jnp.bfloat16)[None],
        grad_up.astype(jnp.bfloat16)[None],
        grad_down.astype(jnp.bfloat16)[None],
    )


MESH = pl.DeviceIdType.MESH
F32 = jnp.float32
BF16 = jnp.bfloat16


def dot(left, right, dims=(((1,), (0,)), ((), ()))):
    return lax.dot_general(left, right, dims, preferred_element_type=F32)


def step_kernel(
    slots,
    n_ex,
    cap,
    direct,
    routes_ref,
    probs_ref,
    place_ref,
    xo_ref,
    xt_ref,
    w0_ref,
    w1_ref,
    w2_ref,
    w3_ref,
    w4_ref,
    w5_ref,
    ig_ref,
    gg_ref,
    gu_ref,
    gd_ref,
    wg,
    wu,
    wd,
    sx,
    rx,
    pd,
    pr,
    ret,
    rc,
    pre_g,
    pre_u,
    hid,
    dgu,
    meta,
    raw,
    part_out,
    part_in,
    puts,
    takes,
    sy,
    rety,
    rawy,
    party_out,
    party_in,
    w_sem,
    meta_sem,
    raw_sem,
    part_sem,
    out_send,
    out_recv,
    fwd_send,
    fwd_recv,
    pair_send,
    pair_recv,
    back_send,
    back_recv,
    side_sem,
    outy_send,
    outy_recv,
    backy_send,
    backy_recv,
):
    tok, width = xo_ref.shape
    near = slots // 2
    half_rows = near * cap
    dp, ex = lax.axis_index("dp"), lax.axis_index("expert")
    side = lax.rem(ex, 2)
    planes = n_ex // 2
    group = slots // planes
    z = lax.div(ex, 2)
    z_far = lax.rem(z + planes // 2, planes)
    me = dp * planes + z
    me_far = dp * planes + z_far
    partner = (dp, 2 * z + 1 - side)
    twin = (dp, 2 * z_far + side)
    cross = (dp, 2 * z_far + 1 - side)

    middle = direct + pl.cdiv(width - direct, 512) * 256
    spans = ([(0, direct)] if direct else []) + [(direct, middle), (middle, width)]
    paired = [i for i, span in enumerate(spans) if span[0] >= direct]
    n_span = len(spans)
    first, second = paired

    def other(i):
        mask = lax.rem(i, group) * planes + lax.div(i, group)
        slot, power = 0, 1
        while power < slots:
            bit = lax.rem(lax.rem(lax.div(me, power), 2) + lax.rem(lax.div(mask, power), 2), 2)
            slot, power = slot + bit * power, 2 * power
        return slot

    def peer(o):
        unit = 2 * other(lax.rem(o, near)) + side
        return (lax.div(unit, n_ex), lax.rem(unit, n_ex))

    def chunk(index):
        return pl.ds(pl.multiple_of(index * cap, cap), cap)

    def each(low, high, body):
        def step(o, carry):
            body(o)
            return carry

        lax.fori_loop(low, high, step, 0)

    def each_down(low, high, body):
        each(0, high - low, lambda o: body(high - 1 - o))

    def columns(body, low=0, high=width, tile=256):
        each(
            low // tile, high // tile, lambda i: body(pl.ds(pl.multiple_of(i * tile, tile), tile))
        )

    def remote(source, target, send, recv, device):
        return pltpu.make_async_remote_copy(
            src_ref=source,
            dst_ref=target,
            send_sem=send,
            recv_sem=recv,
            device_id=device,
            device_id_type=MESH,
        )

    barrier = pltpu.get_barrier_semaphore()
    each(
        1,
        near,
        lambda o: pl.semaphore_signal(barrier, inc=1, device_id=peer(o), device_id_type=MESH),
    )
    for device in (partner, twin, cross):
        pl.semaphore_signal(barrier, inc=1, device_id=device, device_id_type=MESH)

    weight_copies = [
        pltpu.make_async_copy(source, target, w_sem.at[i])
        for i, (source, target) in enumerate(
            [
                (w0_ref, wg.at[0]),
                (w1_ref, wu.at[0]),
                (w2_ref, wd.at[0]),
                (w3_ref, wg.at[1]),
                (w4_ref, wu.at[1]),
                (w5_ref, wd.at[1]),
            ]
        )
    ]
    for copy in weight_copies:
        copy.start()

    def one_hot(compare):
        return jnp.where(compare, 1.0, 0.0).astype(BF16)

    def stand(line):
        size = line.shape[1]
        here = [lax.broadcasted_iota(jnp.int32, (size, size), d) for d in range(2)]
        return jnp.sum(jnp.where(here[0] == here[1], line, 0.0), axis=1, keepdims=True)

    def count(mask, axis):
        return jnp.sum(jnp.where(mask, 1.0, 0.0), axis=axis, keepdims=True)

    meta[0, 0:2, :] = routes_ref[...].astype(F32)
    meta[0, 2:4, :] = probs_ref[...]
    meta[0, 4:8, :] = jnp.zeros((4, tok), F32)

    def meta_copy(block):
        device = (twin, partner, cross)[block - 1]
        sem = meta_sem.at[0, block - 1], meta_sem.at[1, block - 1]
        return remote(meta.at[0], meta.at[block], *sem, device)

    def order_of(slot, home):
        mask = slot.astype(jnp.int32) ^ home
        return lax.rem(mask, planes) * group + lax.div(mask, planes)

    def tables(block):
        home = me_far if block % 2 else me
        low = half_rows * (block % 2)
        down, across = [lax.broadcasted_iota(jnp.int32, (tok, tok), d) for d in range(2)]
        line = [meta[block, k : k + 1, :] for k in range(2)]
        tall = [stand(line[k]) for k in range(2)]
        place = place_ref[...].astype(F32)
        place_tall = stand(place)
        ids_line = lax.broadcasted_iota(jnp.int32, (tok, slots), 1).astype(F32)
        ids_tall = lax.broadcasted_iota(jnp.int32, (slots, tok), 0).astype(F32)
        row_iota = lax.broadcasted_iota(jnp.int32, (half_rows, tok), 0) + low
        col_iota = lax.broadcasted_iota(jnp.int32, (tok, half_rows), 1) + low
        for k in range(2):
            alike = (line[k] == tall[0]) | (line[k] == tall[1])
            slot = jnp.sum(jnp.where(ids_tall == line[k], place_tall, 0.0), axis=0, keepdims=True)
            before = count(alike & (down < across), 0).astype(jnp.int32)
            puts[block, k] = one_hot(row_iota == order_of(slot, home) * cap + before)
            alike = (tall[k] == line[0]) | (tall[k] == line[1])
            slot = jnp.sum(jnp.where(ids_line == tall[k], place, 0.0), axis=1, keepdims=True)
            before = count(alike & (across < down), 1).astype(jnp.int32)
            takes[block, k] = one_hot(col_iota == order_of(slot, home) * cap + before)

    def probs_of(block):
        return [stand(meta[block, 2 + k : 3 + k, :]) for k in range(2)]

    def rows_of(block):
        return pl.ds(half_rows * (block % 2), half_rows)

    def place_rows(target, block, source, low, high):
        put = puts[block, 0] + puts[block, 1]

        def body(cols):
            target[rows_of(block), cols] = dot(put, source[:, cols]).astype(BF16)

        columns(body, low, high)

    def span_of(step):
        return (0, width) if step < 2 else spans[step - 2]

    def into(step):
        return rx.at[step] if step < 2 else rc

    def out_copy(step, o):
        low, high = span_of(step)
        cols = pl.ds(low, high - low)
        return remote(
            sx.at[min(step, 2), chunk(o), cols],
            into(step).at[0, chunk(o), cols],
            out_send.at[step, o],
            out_recv.at[step, o],
            peer(o),
        )

    def fwd_copy(step, o):
        low, high = span_of(step)
        low = max(low, direct)
        here = into(step)
        cols = pl.ds(low, high - low)
        return remote(
            here.at[0, chunk(o), cols],
            here.at[1, chunk(o), cols],
            fwd_send.at[step, o],
            fwd_recv.at[step, o],
            partner,
        )

    forwarded = [0, 1] + [2 + i for i in paired]

    def begin(step, block):
        base = near * block
        each(base + 1, base + near, lambda o: out_copy(step, o).start())
        low, high = span_of(step)
        cols = pl.ds(low, high - low)
        into(step)[0, pl.ds(base * cap, cap), cols] = sx[min(step, 2), pl.ds(base * cap, cap), cols]
        if step in forwarded:
            fwd_copy(step, base).start()

    def relay(step, low, high):
        def body(o):
            out_copy(step, o).wait_recv()
            if step in forwarded:
                fwd_copy(step, o).start()

        each(low, high, body)

    def arrived(step, block):
        each(near * block, near * block + near, lambda o: fwd_copy(step, o).wait_recv())

    def outy_copy(step, o):
        target = rx.at[step] if step < 2 else rc
        return remote(
            sy.at[step, chunk(o)],
            target.at[1, chunk(o), pl.ds(0, direct)],
            outy_send.at[step, o],
            outy_recv.at[step, o],
            peer(o),
        )

    def beginy(step, block):
        base = near * block
        each(base + 1, base + near, lambda o: outy_copy(step, o).start())
        target = rx.at[step] if step < 2 else rc
        target[1, pl.ds(base * cap, cap), 0:direct] = sy[step, pl.ds(base * cap, cap)]

    def arrivedy(step, block):
        each(near * block + 1, near * block + near, lambda o: outy_copy(step, o).wait_recv())

    def raw_copy(step):
        low, high = span_of(step)
        cols = pl.ds(low, high - low)
        source = (xo_ref, xt_ref)[step] if step < 2 else part_out.at[2]
        return remote(
            source.at[:, cols],
            raw.at[min(step, 2), :, cols],
            raw_sem.at[0, step],
            raw_sem.at[1, step],
            twin,
        )

    def side_copy(step, block):
        cols = pl.ds(0, direct)
        source = (xo_ref, xt_ref, part_out.at[2])[step] if block == 0 else raw.at[step]
        return remote(
            source.at[:, cols],
            rawy.at[step, block],
            side_sem.at[0, 2 * step + block],
            side_sem.at[1, 2 * step + block],
            partner,
        )

    def half_cols(turn):
        low, high = spans[turn % n_span]
        return pl.ds(low, high - low)

    def pair_copy(turn, o):
        return remote(
            pd.at[1, chunk(o), half_cols(turn)],
            pr.at[turn // n_span, chunk(o), half_cols(turn)],
            pair_send.at[turn, o],
            pair_recv.at[turn, o],
            partner,
        )

    def back_copy(turn, o):
        return remote(
            pd.at[0, chunk(o), half_cols(turn)],
            ret.at[turn // n_span, chunk(o), half_cols(turn)],
            back_send.at[turn, o],
            back_recv.at[turn, o],
            peer(o),
        )

    def backy_copy(way, o):
        return remote(
            pd.at[1, chunk(o), pl.ds(0, direct)],
            rety.at[way, chunk(o)],
            backy_send.at[way, o],
            backy_recv.at[way, o],
            peer(o),
        )

    def add_part(turn, o):
        pair_copy(turn, o).wait_recv()
        cols = half_cols(turn)
        total = pd[0, chunk(o), cols].astype(F32) + pr[turn // n_span, chunk(o), cols].astype(F32)
        return total.astype(BF16)

    def give_back(turn, block):
        base = near * block

        def body(o):
            pd[0, chunk(o), half_cols(turn)] = add_part(turn, o)
            back_copy(turn, o).start()

        each_down(base + 1, base + near, body)
        ret[turn // n_span, pl.ds(base * cap, cap), half_cols(turn)] = add_part(turn, base)

    def give_direct(way, block):
        base, turn = near * block, n_span * way

        def body(o):
            back_copy(turn, o).start()
            backy_copy(way, o).start()

        each_down(base + 1, base + near, body)
        own = pl.ds(base * cap, cap)
        ret[way, own, 0:direct] = pd[0, own, 0:direct]
        rety[way, own] = pd[1, own, 0:direct]

    def back_came(turn, block):
        each(near * block + 1, near * block + near, lambda o: back_copy(turn, o).wait_recv())

    def backy_came(way, block):
        each(near * block + 1, near * block + near, lambda o: backy_copy(way, o).wait_recv())

    def part_copy(turn):
        way, cols = turn // n_span, half_cols(turn)
        return remote(
            part_out.at[way, :, cols],
            part_in.at[way, :, cols],
            part_sem.at[0, turn],
            part_sem.at[1, turn],
            twin,
        )

    def party_copy(way, block):
        return remote(
            party_out.at[way, block],
            party_in.at[way, block],
            side_sem.at[0, 6 + 2 * way + block],
            side_sem.at[1, 6 + 2 * way + block],
            partner,
        )

    def picked(way, block, source):
        if way == 0:
            p0, p1 = probs_of(block)
            return p0 * dot(takes[block, 0], source) + p1 * dot(takes[block, 1], source)
        return dot(takes[block, 0] + takes[block, 1], source)

    def send_side(way, block):
        backy_came(way, block)
        rows = rows_of(block)

        def body(cols):
            party_out[way, block, :, cols] = picked(way, 2 + block, rety[way, rows, cols]).astype(
                BF16
            )

        columns(body, 0, direct)
        party_copy(way, block).start()

    def send_part(turn):
        way = turn // n_span
        straight = spans[turn % n_span][0] < direct
        back_came(turn, 1)
        if straight:
            party_copy(way, 1).wait_recv()

        def body(cols):
            total = picked(way, 1, ret[way, rows_of(1), cols])
            if straight:
                total = total + party_in[way, 1, :, cols].astype(F32)
            part_out[way, :, cols] = total.astype(BF16)

        columns(body, *spans[turn % n_span])
        part_copy(turn).start()

    def whole(turn, use):
        way = turn // n_span
        straight = spans[turn % n_span][0] < direct
        back_came(turn, 0)
        if straight:
            party_copy(way, 0).wait_recv()
        part_copy(turn).wait_recv()

        def body(cols):
            total = picked(way, 0, ret[way, rows_of(0), cols])
            total = total + part_in[way, :, cols].astype(F32)
            if straight:
                total = total + party_in[way, 0, :, cols].astype(F32)
            use(cols, total)

        columns(body, *spans[turn % n_span])

    def cotangents(block, diff):
        p0, p1 = probs_of(block)
        rows0, rows1 = (p0 * diff).astype(BF16), (p1 * diff).astype(BF16)
        return (dot(puts[block, 0], rows0) + dot(puts[block, 1], rows1)).astype(BF16)

    def own_cotangents(index):
        def use(cols, diff):
            part_out[2, :, cols] = diff.astype(BF16)
            sx[2, rows_of(0), cols] = cotangents(0, diff)

        whole(index, use)
        raw_copy(2 + index).start()
        if spans[index][0] < direct:
            side_copy(2, 0).start()
        begin(2 + index, 0)

    def twin_cotangents(index):
        raw_copy(2 + index).wait_recv()
        if spans[index][0] < direct:
            side_copy(2, 1).start()

        def body(cols):
            sx[2, rows_of(1), cols] = cotangents(1, raw[2, :, cols].astype(F32))

        columns(body, *spans[index])
        begin(2 + index, 1)

    def side_cotangents(block):
        side_copy(2, block).wait_recv()

        def body(cols):
            sy[2, rows_of(block), cols] = cotangents(2 + block, rawy[2, block, :, cols].astype(F32))

        columns(body, 0, direct)
        beginy(2, block)

    def side_inputs(net, block):
        side_copy(net, block).wait_recv()
        place_rows(sy.at[net], 2 + block, rawy.at[net, block], 0, direct)
        beginy(net, block)

    def forward(net, part, block):
        rows = rows_of(block)
        gate = dot(rx[net, part, rows], wg[net])
        up = dot(rx[net, part, rows], wu[net])
        hid[net, part, rows] = (gate * jax.nn.sigmoid(gate) * up).astype(BF16)
        if net == 0:
            pre_g[part, rows] = gate
            pre_u[part, rows] = up

    tables(0)
    place_rows(sx.at[0], 0, xo_ref, 0, width)
    pl.semaphore_wait(barrier, near + 2)
    for block in (1, 2, 3):
        meta_copy(block).start()
    raw_copy(0).start()
    begin(0, 0)
    if direct:
        side_copy(0, 0).start()
    place_rows(sx.at[1], 0, xt_ref, 0, width)
    begin(1, 0)
    if direct:
        side_copy(1, 0).start()
    relay(0, 1, near // 2)
    for block in (2, 1, 3):
        meta_copy(block).wait_recv()
    if direct:
        tables(2)
        side_inputs(0, 0)
    relay(0, near // 2, near)
    tables(1)
    if direct:
        side_inputs(1, 0)
    relay(1, 1, near // 2)
    raw_copy(0).wait_recv()
    raw_copy(0).wait_send()
    raw_copy(1).start()
    place_rows(sx.at[0], 1, raw.at[0], 0, width)
    begin(0, 1)
    if direct:
        side_copy(0, 1).start()
        tables(3)
    relay(1, near // 2, near)
    for copy in weight_copies:
        copy.wait()
    forward(0, 0, 0)
    relay(0, near + 1, slots)
    if direct:
        side_inputs(0, 1)
    raw_copy(1).wait_recv()
    place_rows(sx.at[1], 1, raw.at[1], 0, width)
    begin(1, 1)
    if direct:
        side_copy(1, 1).start()

    def landed(step, block):
        arrived(step, block)
        if direct and step < 2:
            arrivedy(step, block)

    forward(1, 0, 0)
    forward(0, 0, 1)
    landed(0, 0)
    forward(0, 1, 0)
    relay(1, near + 1, slots)
    if direct:
        side_inputs(1, 1)
    forward(1, 0, 1)
    landed(0, 1)
    forward(0, 1, 1)

    def outputs(index, part, block):
        rows = rows_of(block)

        def body(cols):
            diff = dot(hid[0, part, rows], wd[0, :, cols]) - dot(hid[1, part, rows], wd[1, :, cols])
            pd[part, rows, cols] = diff.astype(BF16)

        columns(body, *spans[index])

    def row_grads(index, part, block):
        rows = rows_of(block)

        def body(cols):
            total = dot(dgu[0, part, rows], wg[0, cols, :], contract_last)
            total = total + dot(dgu[1, part, rows], wu[0, cols, :], contract_last)
            pd[part, rows, cols] = total.astype(BF16)

        columns(body, *spans[index])

    def exchange(rows_out, way, block, index):
        rows_out(index, 1, block)
        turn = n_span * way + index
        each_down(near * block, near * block + near, lambda o: pair_copy(turn, o).start())

    def way_back(rows_out, way, ready):
        for block in (0, 1):
            ready(block)
            if direct:
                for part in (0, 1):
                    rows_out(0, part, block)
                give_direct(way, block)
            exchange(rows_out, way, block, first)
        for block in (0, 1):
            rows_out(first, 0, block)
        if direct:
            send_side(way, 1)
            send_side(way, 0)
        for block in (1, 0):
            exchange(rows_out, way, block, second)
        for block in (1, 0):
            rows_out(second, 0, block)

    def ready_outputs(block):
        landed(1, block)
        forward(1, 1, block)

    way_back(outputs, 0, ready_outputs)
    give_back(first, 0)
    give_back(first, 1)
    if direct:
        send_part(0)
    send_part(first)
    if direct:
        own_cotangents(0)
    give_back(second, 1)
    own_cotangents(first)
    if direct:
        twin_cotangents(0)
    send_part(second)
    give_back(second, 0)
    relay(2 + first, 1, near)
    twin_cotangents(first)
    own_cotangents(second)
    if direct:
        side_cotangents(0)
    relay(2 + first, near + 1, slots)
    relay(2 + second, 1, near)
    if direct:
        side_cotangents(1)
    twin_cotangents(second)
    relay(2 + second, near + 1, slots)
    if direct:
        relay(2, 1, near)
        relay(2, near + 1, slots)

    def hidden_back(part, block):
        rows = rows_of(block)
        d_hidden = dot(rc[part, rows], wd[0], contract_last)
        gate, up = pre_g[part, rows], pre_u[part, rows]
        sig = jax.nn.sigmoid(gate)
        dgu[0, part, rows] = (d_hidden * up * sig * (1.0 + gate * (1.0 - sig))).astype(BF16)
        dgu[1, part, rows] = (d_hidden * (gate * sig)).astype(BF16)

    for index in paired:
        each(0, slots, lambda o, index=index: pair_copy(index, o).wait_send())
    for index in range(n_span):
        for base in (0, near):
            each(base + 1, base + near, lambda o, index=index: back_copy(index, o).wait_send())
    if direct:
        for base in (0, near):
            each(base + 1, base + near, lambda o: backy_copy(0, o).wait_send())
    hidden_back(0, 0)
    hidden_back(0, 1)

    def ready_grads(block):
        if direct:
            arrivedy(2, block)
        for index in paired:
            arrived(2 + index, block)
        hidden_back(1, block)

    way_back(row_grads, 1, ready_grads)

    def weight_grads(cols):
        for index, target in ((0, gg_ref), (1, gu_ref)):
            total = dot(rx[0, 0, :, cols], dgu[index, 0], contract_first)
            total = total + dot(rx[0, 1, :, cols], dgu[index, 1], contract_first)
            target[cols, :] = total.astype(BF16)
        total = dot(hid[0, 0], rc[0, :, cols], contract_first)
        total = total + dot(hid[0, 1], rc[1, :, cols], contract_first)
        gd_ref[:, cols] = total.astype(BF16)

    def inputs_grad(cols, total):
        ig_ref[:, cols] = total.astype(BF16)

    columns(weight_grads, 0, width, 512)
    give_back(n_span + first, 0)
    give_back(n_span + first, 1)
    if direct:
        send_part(n_span)
    send_part(n_span + first)
    if direct:
        whole(n_span, inputs_grad)
    give_back(n_span + second, 1)
    send_part(n_span + second)
    whole(n_span + first, inputs_grad)
    give_back(n_span + second, 0)

    for step in range(2 + n_span):
        if step != 0:
            raw_copy(step).wait_send()
        for base in (0, near):
            each(base + 1, base + near, lambda o, step=step: out_copy(step, o).wait_send())
        if step in forwarded:
            each(0, slots, lambda o, step=step: fwd_copy(step, o).wait_send())
    for block in (1, 2, 3):
        meta_copy(block).wait_send()
    for turn in range(2 * n_span):
        part_copy(turn).wait_send()
    if direct:
        for step in range(3):
            for block in (0, 1):
                side_copy(step, block).wait_send()
            for base in (0, near):
                each(base + 1, base + near, lambda o, step=step: outy_copy(step, o).wait_send())
        for way in (0, 1):
            for block in (0, 1):
                party_copy(way, block).wait_send()
    whole(n_span + second, inputs_grad)
    for index in paired:
        each(0, slots, lambda o, index=index: pair_copy(n_span + index, o).wait_send())
    for index in range(n_span):
        for base in (0, near):
            each(
                base + 1, base + near, lambda o, index=index: back_copy(n_span + index, o).wait_send()
            )
    if direct:
        for base in (0, near):
            each(base + 1, base + near, lambda o: backy_copy(1, o).wait_send())


def hand_over(pieces, *refs):
    come, leave = refs[12], refs[13]
    given, taken = [], []
    for i in range(4):
        size = refs[i].shape[0] // pieces
        for piece in range(pieces):
            rows = pl.ds(piece * size, size)
            held = refs[8 + i].at[rows]
            given.append(pltpu.make_async_copy(refs[i].at[rows], held, come.at[i, piece]))
            taken.append(pltpu.make_async_copy(held, refs[4 + i].at[rows], leave.at[i, piece]))
    for copy in given:
        copy.start()
    for copy, later in zip(given, taken):
        copy.wait()
        later.start()
    for copy in taken:
        copy.wait()


def shards(
    x_online,
    x_target,
    routes,
    gate_probs,
    expert_place,
    gate_online,
    up_online,
    down_online,
    gate_target,
    up_target,
    down_target,
):
    tok, width = x_online.shape
    slots = expert_place.shape[0]
    n_ex = lax.axis_size("expert")
    cap = 2 * ((2 * tok + slots - 1) // slots)
    rows = slots * cap
    half = gate_online.shape[2]
    paired = 2 * slots == lax.axis_size("dp") * n_ex and n_ex % 2 == 0
    halving = slots & (slots - 1) == 0 and n_ex & (n_ex - 1) == 0
    if cap % 16 or width % 1024 or tok % 128 or slots < 16 or n_ex < 4 or not (paired and halving):
        return shards_plain(
            x_online,
            x_target,
            routes,
            gate_probs,
            expert_place,
            gate_online,
            up_online,
            down_online,
            gate_target,
            up_target,
            down_target,
        )
    direct = 256
    n_span = 3 if direct else 2
    side_cols = max(direct, 128)
    near = slots // 2
    vmem = pl.BlockSpec(memory_space=pltpu.VMEM)
    hbm = pl.BlockSpec(memory_space=pl.ANY)
    dma = pltpu.SemaphoreType.DMA
    outs = pl.pallas_call(
        functools.partial(step_kernel, slots, n_ex, cap, direct),
        out_shape=(
            jax.ShapeDtypeStruct((tok, width), BF16),
            jax.ShapeDtypeStruct((width, half), BF16),
            jax.ShapeDtypeStruct((width, half), BF16),
            jax.ShapeDtypeStruct((half, width), BF16),
        ),
        in_specs=[vmem] * 5 + [hbm] * 6,
        out_specs=(vmem,) * 4,
        scratch_shapes=[
            pltpu.VMEM((2, width, half), BF16),
            pltpu.VMEM((2, width, half), BF16),
            pltpu.VMEM((2, half, width), BF16),
            pltpu.VMEM((3, rows, width), BF16),
            pltpu.VMEM((2, 2, rows, width), BF16),
            pltpu.VMEM((2, rows, width), BF16),
            pltpu.VMEM((2, rows, width), BF16),
            pltpu.VMEM((2, rows, width), BF16),
            pltpu.VMEM((2, rows, width), BF16),
            pltpu.VMEM((2, rows, half), F32),
            pltpu.VMEM((2, rows, half), F32),
            pltpu.VMEM((2, 2, rows, half), BF16),
            pltpu.VMEM((2, 2, rows, half), BF16),
            pltpu.VMEM((4, 8, tok), F32),
            pltpu.VMEM((3, tok, width), BF16),
            pltpu.VMEM((3, tok, width), BF16),
            pltpu.VMEM((2, tok, width), BF16),
            pltpu.VMEM((4, 2, near * cap, tok), BF16),
            pltpu.VMEM((4, 2, tok, near * cap), BF16),
            pltpu.VMEM((3, rows, side_cols), BF16),
            pltpu.VMEM((2, rows, side_cols), BF16),
            pltpu.VMEM((3, 2, tok, side_cols), BF16),
            pltpu.VMEM((2, 2, tok, side_cols), BF16),
            pltpu.VMEM((2, 2, tok, side_cols), BF16),
            dma((6,)),
            dma((2, 3)),
            dma((2, 2 + n_span)),
            dma((2, 2 * n_span)),
            dma((2 + n_span, slots)),
            dma((2 + n_span, slots)),
            dma((2 + n_span, slots)),
            dma((2 + n_span, slots)),
            dma((2 * n_span, slots)),
            dma((2 * n_span, slots)),
            dma((2 * n_span, slots)),
            dma((2 * n_span, slots)),
            dma((2, 10)),
            dma((3, slots)),
            dma((3, slots)),
            dma((2, slots)),
            dma((2, slots)),
        ],
        compiler_params=pltpu.CompilerParams(
            collective_id=0, has_side_effects=True, vmem_limit_bytes=60 * 2**20
        ),
    )(
        routes.T,
        gate_probs.T,
        expert_place[None],
        x_online,
        x_target,
        gate_online[0],
        up_online[0],
        down_online[0],
        gate_target[0],
        up_target[0],
        down_target[0],
    )
    pieces = 4
    outs = pl.pallas_call(
        functools.partial(hand_over, pieces),
        out_shape=tuple(jax.ShapeDtypeStruct(o.shape, o.dtype) for o in outs),
        in_specs=[hbm] * 4,
        out_specs=(hbm,) * 4,
        scratch_shapes=[pltpu.VMEM(o.shape, o.dtype) for o in outs]
        + [dma((4, pieces)), dma((4, pieces))],
    )(*outs)
    return (outs[0], outs[1][None], outs[2][None], outs[3][None])


def solution(mesh):
    in_specs = (
        P(("dp", "expert"), None),
        P(("dp", "expert"), None),
        P(("dp", "expert"), None),
        P(("dp", "expert"), None),
        P(),
        P(("dp", "expert"), None, None),
        P(("dp", "expert"), None, None),
        P(("dp", "expert"), None, None),
        P(("dp", "expert"), None, None),
        P(("dp", "expert"), None, None),
        P(("dp", "expert"), None, None),
    )
    out_specs = (
        P(("dp", "expert"), None),
        P(("dp", "expert"), None, None),
        P(("dp", "expert"), None, None),
        P(("dp", "expert"), None, None),
    )
    return jax.shard_map(shards, mesh=mesh, in_specs=in_specs, out_specs=out_specs, check_vma=False)
```

```python
import functools

import jax
import jax.numpy as jnp
from jax import lax
from jax.experimental import pallas as pl
from jax.experimental.pallas import tpu as pltpu
from jax.sharding import PartitionSpec as P

contract_last = (((1,), (1,)), ((), ()))
contract_first = (((0,), (0,)), ((), ()))


def swapped(block, axis, bit):
    count = lax.axis_size(axis)
    route = []
    for low in range(count):
        high = low | 1 << bit
        if high != low and high < count:
            route += [(low, high), (high, low)]
    return lax.ppermute(block, axis, route)


def hidden_forward(inputs, w_gate, w_up):
    pre_gate = jnp.dot(inputs, w_gate, preferred_element_type=jnp.float32)
    pre_up = jnp.dot(inputs, w_up, preferred_element_type=jnp.float32)
    hidden = (jax.nn.silu(pre_gate) * pre_up).astype(jnp.bfloat16)
    return (pre_gate, pre_up, hidden)


def hidden_grads(cotangent, pre_gate, pre_up, w_down):
    d_hidden = lax.dot_general(cotangent, w_down, contract_last, preferred_element_type=jnp.float32)
    sigmoid_gate = jax.nn.sigmoid(pre_gate)
    d_gate = (d_hidden * pre_up * sigmoid_gate * (1.0 + pre_gate * (1.0 - sigmoid_gate))).astype(
        jnp.bfloat16
    )
    d_up = (d_hidden * jax.nn.silu(pre_gate)).astype(jnp.bfloat16)
    return (d_gate, d_up)


def input_rows(d_gate, d_up, w_gate, w_up):
    total = lax.dot_general(d_gate, w_gate, contract_last, preferred_element_type=jnp.float32)
    total = total + lax.dot_general(d_up, w_up, contract_last, preferred_element_type=jnp.float32)
    return total.astype(jnp.bfloat16)


def outer_sum(left, right):
    return lax.dot_general(left, right, contract_first, preferred_element_type=jnp.float32)


def earlier_same(chosen):
    turn = jnp.arange(chosen.shape[0], dtype=jnp.int32)
    alike = (chosen[:, None] == chosen[None, :]) & (turn[None, :] < turn[:, None])
    return jnp.sum(alike.astype(jnp.int32), axis=1)


def shards_plain(
    x_online,
    x_target,
    routes,
    gate_probs,
    expert_place,
    gate_online,
    up_online,
    down_online,
    gate_target,
    up_target,
    down_target,
):
    tok_rows, model_width = x_online.shape
    dp_count = lax.axis_size("dp")
    expert_count = lax.axis_size("expert")
    unit_count = dp_count * expert_count
    experts = expert_place.shape[0]
    capacity = 2 * ((2 * tok_rows + experts - 1) // experts)
    half_cap = capacity // 2
    half_width = gate_online.shape[2]
    chosen = routes.reshape(-1)
    onehot = (chosen[:, None] == jnp.arange(experts, dtype=jnp.int32)[None, :]).astype(jnp.int32)
    position = earlier_same(chosen)
    slot_place = jnp.sum(onehot * expert_place[None, :], axis=1)
    flat_slot = (2 * slot_place + position // half_cap) * half_cap + position % half_cap
    owner_token = jnp.arange(2 * tok_rows, dtype=jnp.int32) // 2

    def to_units(source):
        blank_rows = jnp.zeros((unit_count * half_cap, model_width), source.dtype)
        return (
            blank_rows.at[flat_slot]
            .set(source)
            .reshape(dp_count, expert_count, half_cap, model_width)
        )

    def from_units(block):
        picked = block.reshape(unit_count * half_cap, model_width)[flat_slot]
        return picked.astype(jnp.float32).reshape(tok_rows, 2, model_width)

    partner = swapped(
        (gate_online, up_online, down_online, gate_target, up_target, down_target), "expert", 0
    )
    gate_full = jnp.concatenate([gate_online[0], partner[0][0]], axis=1)
    up_full = jnp.concatenate([up_online[0], partner[1][0]], axis=1)
    down_full = jnp.concatenate([down_online[0], partner[2][0]], axis=0)
    gate_tfull = jnp.concatenate([gate_target[0], partner[3][0]], axis=1)
    up_tfull = jnp.concatenate([up_target[0], partner[4][0]], axis=1)
    down_tfull = jnp.concatenate([down_target[0], partner[5][0]], axis=0)
    recv_online, recv_target = (
        lax.all_to_all(
            lax.all_to_all(
                to_units(x_online[owner_token]), "dp", split_axis=0, concat_axis=0, tiled=True
            ),
            "expert",
            split_axis=1,
            concat_axis=1,
            tiled=True,
        ),
        lax.all_to_all(
            lax.all_to_all(
                to_units(x_target[owner_token]), "dp", split_axis=0, concat_axis=0, tiled=True
            ),
            "expert",
            split_axis=1,
            concat_axis=1,
            tiled=True,
        ),
    )
    unit_shape = recv_online.shape
    inputs_online = recv_online.reshape(-1, model_width)
    inputs_target = recv_target.reshape(-1, model_width)
    pre_gate, pre_up, hidden = hidden_forward(inputs_online, gate_full, up_full)
    out_online = jnp.dot(hidden, down_full, preferred_element_type=jnp.float32).astype(jnp.bfloat16)
    hidden_target = hidden_forward(inputs_target, gate_tfull, up_tfull)[2]
    out_target = jnp.dot(hidden_target, down_tfull, preferred_element_type=jnp.float32).astype(
        jnp.bfloat16
    )
    back_online, back_target = (
        lax.all_to_all(
            lax.all_to_all(
                out_online.reshape(unit_shape), "dp", split_axis=0, concat_axis=0, tiled=True
            ),
            "expert",
            split_axis=1,
            concat_axis=1,
            tiled=True,
        ),
        lax.all_to_all(
            lax.all_to_all(
                out_target.reshape(unit_shape), "dp", split_axis=0, concat_axis=0, tiled=True
            ),
            "expert",
            split_axis=1,
            concat_axis=1,
            tiled=True,
        ),
    )
    y_online = jnp.sum(from_units(back_online) * gate_probs[:, :, None], axis=1)
    y_target = jnp.sum(from_units(back_target) * gate_probs[:, :, None], axis=1)
    cotangent = (
        (gate_probs[:, :, None] * (y_online - y_target)[:, None, :])
        .astype(jnp.bfloat16)
        .reshape(2 * tok_rows, model_width)
    )
    cot_recv = lax.all_to_all(
        lax.all_to_all(to_units(cotangent), "dp", split_axis=0, concat_axis=0, tiled=True),
        "expert",
        split_axis=1,
        concat_axis=1,
        tiled=True,
    )
    cot_rows = cot_recv.reshape(-1, model_width)
    d_gate, d_up = hidden_grads(cot_rows, pre_gate, pre_up, down_full)
    d_rows = input_rows(d_gate, d_up, gate_full, up_full)
    back_grads = lax.all_to_all(
        lax.all_to_all(d_rows.reshape(unit_shape), "dp", split_axis=0, concat_axis=0, tiled=True),
        "expert",
        split_axis=1,
        concat_axis=1,
        tiled=True,
    )
    input_grad = jnp.sum(from_units(back_grads), axis=1).astype(jnp.bfloat16)
    g_gate = outer_sum(inputs_online, d_gate)
    g_up = outer_sum(inputs_online, d_up)
    g_down = outer_sum(hidden, cot_rows)
    sent = (
        swapped(g_gate[:, half_width:].astype(jnp.bfloat16), "expert", 0).astype(jnp.float32),
        swapped(g_up[:, half_width:].astype(jnp.bfloat16), "expert", 0).astype(jnp.float32),
        swapped(g_down[half_width:].astype(jnp.bfloat16), "expert", 0).astype(jnp.float32),
    )
    grad_gate = g_gate[:, :half_width] + sent[0]
    grad_up = g_up[:, :half_width] + sent[1]
    grad_down = g_down[:half_width] + sent[2]
    return (
        input_grad,
        grad_gate.astype(jnp.bfloat16)[None],
        grad_up.astype(jnp.bfloat16)[None],
        grad_down.astype(jnp.bfloat16)[None],
    )


MESH = pl.DeviceIdType.MESH
F32 = jnp.float32
BF16 = jnp.bfloat16


def dot(left, right, dims=(((1,), (0,)), ((), ()))):
    return lax.dot_general(left, right, dims, preferred_element_type=F32)


def step_kernel(
    slots,
    n_ex,
    cap,
    direct,
    routes_ref,
    probs_ref,
    place_ref,
    xo_hbm,
    xt_hbm,
    w0_ref,
    w1_ref,
    w2_ref,
    w3_ref,
    w4_ref,
    w5_ref,
    ig_hbm,
    gg_hbm,
    gu_hbm,
    gd_hbm,
    xo_ref,
    xt_ref,
    ig_ref,
    gg_ref,
    gu_ref,
    gd_ref,
    io_sem,
    wg,
    wu,
    wd,
    sx,
    rx,
    pd,
    pr,
    ret,
    rc,
    pre_g,
    pre_u,
    hid,
    dgu,
    meta,
    raw,
    part_out,
    part_in,
    puts,
    takes,
    sy,
    rety,
    rawy,
    party_out,
    party_in,
    w_sem,
    meta_sem,
    raw_sem,
    part_sem,
    out_send,
    out_recv,
    fwd_send,
    fwd_recv,
    pair_send,
    pair_recv,
    back_send,
    back_recv,
    side_sem,
    outy_send,
    outy_recv,
    backy_send,
    backy_recv,
):
    tok, width = xo_ref.shape
    near = slots // 2
    half_rows = near * cap
    dp, ex = lax.axis_index("dp"), lax.axis_index("expert")
    side = lax.rem(ex, 2)
    planes = n_ex // 2
    group = slots // planes
    z = lax.div(ex, 2)
    z_far = lax.rem(z + planes // 2, planes)
    me = dp * planes + z
    me_far = dp * planes + z_far
    partner = (dp, 2 * z + 1 - side)
    twin = (dp, 2 * z_far + side)
    cross = (dp, 2 * z_far + 1 - side)

    middle = direct + (width - direct) // 512 * 256
    spans = ([(0, direct)] if direct else []) + [(direct, middle), (middle, width)]
    paired = [i for i, span in enumerate(spans) if span[0] >= direct]
    n_span = len(spans)
    first, second = paired

    def other(i):
        mask = lax.rem(i, group) * planes + lax.div(i, group)
        slot, power = 0, 1
        while power < slots:
            bit = lax.rem(lax.rem(lax.div(me, power), 2) + lax.rem(lax.div(mask, power), 2), 2)
            slot, power = slot + bit * power, 2 * power
        return slot

    def peer(o):
        unit = 2 * other(lax.rem(o, near)) + side
        return (lax.div(unit, n_ex), lax.rem(unit, n_ex))

    def chunk(index, many=1):
        return pl.ds(pl.multiple_of(index * cap, cap), many * cap)

    def each(low, high, body):
        def step(o, carry):
            body(o)
            return carry

        lax.fori_loop(low, high, step, 0)

    def each_down(low, high, body):
        each(0, high - low, lambda o: body(high - 1 - o))

    def columns(body, low=0, high=width, tile=256):
        each(
            low // tile, high // tile, lambda i: body(pl.ds(pl.multiple_of(i * tile, tile), tile))
        )

    def remote(source, target, send, recv, device):
        return pltpu.make_async_remote_copy(
            src_ref=source,
            dst_ref=target,
            send_sem=send,
            recv_sem=recv,
            device_id=device,
            device_id_type=MESH,
        )

    input_copies = [
        pltpu.make_async_copy(xo_hbm, xo_ref, io_sem.at[0]),
        pltpu.make_async_copy(xt_hbm, xt_ref, io_sem.at[1]),
    ]
    for copy in input_copies:
        copy.start()

    barrier = pltpu.get_barrier_semaphore()
    each(
        1,
        near,
        lambda o: pl.semaphore_signal(barrier, inc=1, device_id=peer(o), device_id_type=MESH),
    )
    for device in (partner, twin, cross):
        pl.semaphore_signal(barrier, inc=1, device_id=device, device_id_type=MESH)

    weight_copies = [
        pltpu.make_async_copy(source, target, w_sem.at[i])
        for i, (source, target) in enumerate(
            [
                (w0_ref, wg.at[0]),
                (w1_ref, wu.at[0]),
                (w2_ref, wd.at[0]),
                (w3_ref, wg.at[1]),
                (w4_ref, wu.at[1]),
                (w5_ref, wd.at[1]),
            ]
        )
    ]
    for copy in weight_copies:
        copy.start()

    def one_hot(compare):
        return jnp.where(compare, 1.0, 0.0).astype(BF16)

    def stand(line):
        size = line.shape[1]
        here = [lax.broadcasted_iota(jnp.int32, (size, size), d) for d in range(2)]
        return jnp.sum(jnp.where(here[0] == here[1], line, 0.0), axis=1, keepdims=True)

    def count(mask, axis):
        return jnp.sum(jnp.where(mask, 1.0, 0.0), axis=axis, keepdims=True)

    meta[0, 0:2, :] = routes_ref[...].astype(F32)
    meta[0, 2:4, :] = probs_ref[...]
    meta[0, 4:8, :] = jnp.zeros((4, tok), F32)

    def meta_copy(block):
        device = (twin, partner, cross)[block - 1]
        sem = meta_sem.at[0, block - 1], meta_sem.at[1, block - 1]
        return remote(meta.at[0], meta.at[block], *sem, device)

    def order_of(slot, home):
        mask = slot.astype(jnp.int32) ^ home
        return lax.rem(mask, planes) * group + lax.div(mask, planes)

    def tables(block):
        home = me_far if block % 2 else me
        low = half_rows * (block % 2)
        down, across = [lax.broadcasted_iota(jnp.int32, (tok, tok), d) for d in range(2)]
        line = [meta[block, k : k + 1, :] for k in range(2)]
        tall = [stand(line[k]) for k in range(2)]
        place = place_ref[...].astype(F32)
        place_tall = stand(place)
        ids_line = lax.broadcasted_iota(jnp.int32, (tok, slots), 1).astype(F32)
        ids_tall = lax.broadcasted_iota(jnp.int32, (slots, tok), 0).astype(F32)
        row_iota = lax.broadcasted_iota(jnp.int32, (half_rows, tok), 0) + low
        col_iota = lax.broadcasted_iota(jnp.int32, (tok, half_rows), 1) + low
        for k in range(2):
            alike = (line[k] == tall[0]) | (line[k] == tall[1])
            slot = jnp.sum(jnp.where(ids_tall == line[k], place_tall, 0.0), axis=0, keepdims=True)
            before = count(alike & (down < across), 0).astype(jnp.int32)
            puts[block, k] = one_hot(row_iota == order_of(slot, home) * cap + before)
            alike = (tall[k] == line[0]) | (tall[k] == line[1])
            slot = jnp.sum(jnp.where(ids_line == tall[k], place, 0.0), axis=1, keepdims=True)
            before = count(alike & (across < down), 1).astype(jnp.int32)
            takes[block, k] = one_hot(col_iota == order_of(slot, home) * cap + before)

    def probs_of(block):
        return [stand(meta[block, 2 + k : 3 + k, :]) for k in range(2)]

    def rows_of(block):
        return pl.ds(half_rows * (block % 2), half_rows)

    def place_rows(target, block, source, low, high):
        put = puts[block, 0] + puts[block, 1]

        def body(cols):
            target[rows_of(block), cols] = dot(put, source[:, cols]).astype(BF16)

        columns(body, low, high)

    def span_of(step):
        return (0, width) if step < 2 else spans[step - 2]

    def into(step):
        return rx.at[step] if step < 2 else rc

    def out_copy(step, o, many=1):
        low, high = span_of(step)
        cols = pl.ds(low, high - low)
        return remote(
            sx.at[min(step, 2), chunk(o, many), cols],
            into(step).at[0, chunk(o, many), cols],
            out_send.at[step, lax.div(o, near)],
            out_recv.at[step, o],
            peer(o),
        )

    def fwd_copy(step, o, many=1):
        low, high = span_of(step)
        low = max(low, direct)
        here = into(step)
        cols = pl.ds(low, high - low)
        return remote(
            here.at[0, chunk(o, many), cols],
            here.at[1, chunk(o, many), cols],
            fwd_send.at[step, lax.div(o, near)],
            fwd_recv.at[step, lax.div(o, near)],
            partner,
        )

    forwarded = [0, 1] + [2 + i for i in paired]

    def begin(step, block):
        base = near * block
        each(base + 1, base + near, lambda o: out_copy(step, o).start())
        low, high = span_of(step)
        cols = pl.ds(low, high - low)
        into(step)[0, pl.ds(base * cap, cap), cols] = sx[min(step, 2), pl.ds(base * cap, cap), cols]
        if step in forwarded:
            fwd_copy(step, base).start()

    def relay(step, low, high):
        def body(o):
            out_copy(step, o).wait_recv()
            if step in forwarded:
                fwd_copy(step, o).start()

        each(low, high, body)

    def arrived(step, block):
        fwd_copy(step, near * block, near).wait_recv()

    def outy_copy(step, o, many=1):
        target = rx.at[step] if step < 2 else rc
        return remote(
            sy.at[step, chunk(o, many)],
            target.at[1, chunk(o, many), pl.ds(0, direct)],
            outy_send.at[step, lax.div(o, near)],
            outy_recv.at[step, lax.div(o, near)],
            peer(o),
        )

    def beginy(step, block):
        base = near * block
        each(base + 1, base + near, lambda o: outy_copy(step, o).start())
        target = rx.at[step] if step < 2 else rc
        target[1, pl.ds(base * cap, cap), 0:direct] = sy[step, pl.ds(base * cap, cap)]

    def arrivedy(step, block):
        outy_copy(step, near * block + 1, near - 1).wait_recv()

    def raw_copy(step):
        low, high = span_of(step)
        cols = pl.ds(low, high - low)
        source = (xo_ref, xt_ref)[step] if step < 2 else part_out.at[2]
        return remote(
            source.at[:, cols],
            raw.at[min(step, 2), :, cols],
            raw_sem.at[0, step],
            raw_sem.at[1, step],
            twin,
        )

    def side_copy(step, block):
        cols = pl.ds(0, direct)
        source = (xo_ref, xt_ref, part_out.at[2])[step] if block == 0 else raw.at[step]
        return remote(
            source.at[:, cols],
            rawy.at[step, block],
            side_sem.at[0, 2 * step + block],
            side_sem.at[1, 2 * step + block],
            partner,
        )

    def half_cols(turn):
        low, high = spans[turn % n_span]
        return pl.ds(low, high - low)

    def paired_turn(turn):
        return 2 * (turn // n_span) + paired.index(turn % n_span)

    def pair_copy(turn, o, many=1):
        return remote(
            pd.at[1, chunk(o, many), half_cols(turn)],
            pr.at[turn // n_span, chunk(o, many), half_cols(turn)],
            pair_send.at[paired_turn(turn), lax.div(o, near)],
            pair_recv.at[paired_turn(turn), o],
            partner,
        )

    def back_copy(turn, o, many=1):
        return remote(
            pd.at[0, chunk(o, many), half_cols(turn)],
            ret.at[turn // n_span, chunk(o, many), half_cols(turn)],
            back_send.at[turn, lax.div(o, near)],
            back_recv.at[turn, lax.div(o, near)],
            peer(o),
        )

    def backy_copy(way, o, many=1):
        return remote(
            pd.at[1, chunk(o, many), pl.ds(0, direct)],
            rety.at[way, chunk(o, many)],
            backy_send.at[way, lax.div(o, near)],
            backy_recv.at[way, lax.div(o, near)],
            peer(o),
        )

    def add_part(turn, o):
        pair_copy(turn, o).wait_recv()
        cols = half_cols(turn)
        total = pd[0, chunk(o), cols].astype(F32) + pr[turn // n_span, chunk(o), cols].astype(F32)
        return total.astype(BF16)

    def give_back(turn, block):
        base = near * block

        def body(o):
            pd[0, chunk(o), half_cols(turn)] = add_part(turn, o)
            back_copy(turn, o).start()

        each_down(base + 1, base + near, body)
        ret[turn // n_span, pl.ds(base * cap, cap), half_cols(turn)] = add_part(turn, base)

    def give_direct(way, block):
        base, turn = near * block, n_span * way

        def body(o):
            back_copy(turn, o).start()
            backy_copy(way, o).start()

        each_down(base + 1, base + near, body)
        own = pl.ds(base * cap, cap)
        ret[way, own, 0:direct] = pd[0, own, 0:direct]
        rety[way, own] = pd[1, own, 0:direct]

    def back_came(turn, block):
        back_copy(turn, near * block + 1, near - 1).wait_recv()

    def backy_came(way, block):
        backy_copy(way, near * block + 1, near - 1).wait_recv()

    def part_copy(turn):
        way, cols = turn // n_span, half_cols(turn)
        return remote(
            part_out.at[way, :, cols],
            part_in.at[way, :, cols],
            part_sem.at[0, turn],
            part_sem.at[1, turn],
            twin,
        )

    def party_copy(way, block):
        return remote(
            party_out.at[way, block],
            party_in.at[way, block],
            side_sem.at[0, 6 + 2 * way + block],
            side_sem.at[1, 6 + 2 * way + block],
            partner,
        )

    def picked(way, block, source):
        if way == 0:
            p0, p1 = probs_of(block)
            return p0 * dot(takes[block, 0], source) + p1 * dot(takes[block, 1], source)
        return dot(takes[block, 0] + takes[block, 1], source)

    def send_side(way, block):
        backy_came(way, block)
        rows = rows_of(block)

        def body(cols):
            party_out[way, block, :, cols] = picked(way, 2 + block, rety[way, rows, cols]).astype(
                BF16
            )

        columns(body, 0, direct)
        party_copy(way, block).start()

    def send_part(turn):
        way = turn // n_span
        straight = spans[turn % n_span][0] < direct
        back_came(turn, 1)
        if straight:
            party_copy(way, 1).wait_recv()

        def body(cols):
            total = picked(way, 1, ret[way, rows_of(1), cols])
            if straight:
                total = total + party_in[way, 1, :, cols].astype(F32)
            part_out[way, :, cols] = total.astype(BF16)

        columns(body, *spans[turn % n_span])
        part_copy(turn).start()

    def whole(turn, use):
        way = turn // n_span
        straight = spans[turn % n_span][0] < direct
        back_came(turn, 0)
        if straight:
            party_copy(way, 0).wait_recv()
        part_copy(turn).wait_recv()

        def body(cols):
            total = picked(way, 0, ret[way, rows_of(0), cols])
            total = total + part_in[way, :, cols].astype(F32)
            if straight:
                total = total + party_in[way, 0, :, cols].astype(F32)
            use(cols, total)

        columns(body, *spans[turn % n_span])

    def cotangents(block, diff):
        p0, p1 = probs_of(block)
        rows0, rows1 = (p0 * diff).astype(BF16), (p1 * diff).astype(BF16)
        return (dot(puts[block, 0], rows0) + dot(puts[block, 1], rows1)).astype(BF16)

    def own_cotangents(index):
        def use(cols, diff):
            part_out[2, :, cols] = diff.astype(BF16)
            sx[2, rows_of(0), cols] = cotangents(0, diff)

        whole(index, use)
        raw_copy(2 + index).start()
        if spans[index][0] < direct:
            side_copy(2, 0).start()
        begin(2 + index, 0)

    def twin_cotangents(index):
        raw_copy(2 + index).wait_recv()
        if spans[index][0] < direct:
            side_copy(2, 1).start()

        def body(cols):
            sx[2, rows_of(1), cols] = cotangents(1, raw[2, :, cols].astype(F32))

        columns(body, *spans[index])
        begin(2 + index, 1)

    def side_cotangents(block):
        side_copy(2, block).wait_recv()

        def body(cols):
            sy[2, rows_of(block), cols] = cotangents(2 + block, rawy[2, block, :, cols].astype(F32))

        columns(body, 0, direct)
        beginy(2, block)

    def side_inputs(net, block):
        side_copy(net, block).wait_recv()
        place_rows(sy.at[net], 2 + block, rawy.at[net, block], 0, direct)
        beginy(net, block)

    def forward(net, part, block):
        rows = rows_of(block)
        gate = dot(rx[net, part, rows], wg[net])
        up = dot(rx[net, part, rows], wu[net])
        hid[net, part, rows] = (gate * jax.nn.sigmoid(gate) * up).astype(BF16)
        if net == 0:
            pre_g[part, rows] = gate
            pre_u[part, rows] = up

    tables(0)
    input_copies[0].wait()
    place_rows(sx.at[0], 0, xo_ref, 0, width)
    pl.semaphore_wait(barrier, near + 2)
    for block in (1, 2, 3):
        meta_copy(block).start()
    raw_copy(0).start()
    begin(0, 0)
    if direct:
        side_copy(0, 0).start()
    input_copies[1].wait()
    place_rows(sx.at[1], 0, xt_ref, 0, width)
    begin(1, 0)
    if direct:
        side_copy(1, 0).start()
    relay(0, 1, near // 2)
    for block in (2, 1, 3):
        meta_copy(block).wait_recv()
    if direct:
        tables(2)
        side_inputs(0, 0)
    relay(0, near // 2, near)
    tables(1)
    if direct:
        side_inputs(1, 0)
    relay(1, 1, near // 2)
    raw_copy(0).wait_recv()
    raw_copy(0).wait_send()
    raw_copy(1).start()
    place_rows(sx.at[0], 1, raw.at[0], 0, width)
    begin(0, 1)
    if direct:
        side_copy(0, 1).start()
        tables(3)
    relay(1, near // 2, near)
    for copy in weight_copies:
        copy.wait()
    forward(0, 0, 0)
    relay(0, near + 1, slots)
    if direct:
        side_inputs(0, 1)
    raw_copy(1).wait_recv()
    place_rows(sx.at[1], 1, raw.at[1], 0, width)
    begin(1, 1)
    if direct:
        side_copy(1, 1).start()

    def landed(step, block):
        arrived(step, block)
        if direct and step < 2:
            arrivedy(step, block)

    forward(1, 0, 0)
    forward(0, 0, 1)
    landed(0, 0)
    forward(0, 1, 0)
    relay(1, near + 1, slots)
    if direct:
        side_inputs(1, 1)
    forward(1, 0, 1)
    landed(0, 1)
    forward(0, 1, 1)

    def outputs(index, part, block):
        rows = rows_of(block)

        def body(cols):
            diff = dot(hid[0, part, rows], wd[0, :, cols]) - dot(hid[1, part, rows], wd[1, :, cols])
            pd[part, rows, cols] = diff.astype(BF16)

        columns(body, *spans[index])

    def row_grads(index, part, block):
        rows = rows_of(block)

        def body(cols):
            total = dot(dgu[0, part, rows], wg[0, cols, :], contract_last)
            total = total + dot(dgu[1, part, rows], wu[0, cols, :], contract_last)
            pd[part, rows, cols] = total.astype(BF16)

        columns(body, *spans[index])

    def exchange(rows_out, way, block, index):
        rows_out(index, 1, block)
        turn = n_span * way + index
        each_down(near * block, near * block + near, lambda o: pair_copy(turn, o).start())

    def way_back(rows_out, way, ready):
        for block in (0, 1):
            ready(block)
            if direct:
                for part in (0, 1):
                    rows_out(0, part, block)
                give_direct(way, block)
            exchange(rows_out, way, block, first)
        for block in (0, 1):
            rows_out(first, 0, block)
        if direct:
            send_side(way, 1)
            send_side(way, 0)
        for block in (1, 0):
            exchange(rows_out, way, block, second)
        for block in (1, 0):
            rows_out(second, 0, block)

    def ready_outputs(block):
        landed(1, block)
        forward(1, 1, block)

    way_back(outputs, 0, ready_outputs)
    give_back(first, 0)
    give_back(first, 1)
    if direct:
        send_part(0)
    send_part(first)
    if direct:
        own_cotangents(0)
    give_back(second, 1)
    own_cotangents(first)
    if direct:
        twin_cotangents(0)
    send_part(second)
    give_back(second, 0)
    relay(2 + first, 1, near)
    twin_cotangents(first)
    own_cotangents(second)
    if direct:
        side_cotangents(0)
    relay(2 + first, near + 1, slots)
    relay(2 + second, 1, near)
    if direct:
        side_cotangents(1)
    twin_cotangents(second)
    relay(2 + second, near + 1, slots)
    if direct:
        relay(2, 1, near)
        relay(2, near + 1, slots)

    def hidden_back(part, block):
        rows = rows_of(block)
        d_hidden = dot(rc[part, rows], wd[0], contract_last)
        gate, up = pre_g[part, rows], pre_u[part, rows]
        sig = jax.nn.sigmoid(gate)
        dgu[0, part, rows] = (d_hidden * up * sig * (1.0 + gate * (1.0 - sig))).astype(BF16)
        dgu[1, part, rows] = (d_hidden * (gate * sig)).astype(BF16)

    def went(way):
        for base in (0, near):
            for index in paired:
                pair_copy(n_span * way + index, base, near).wait_send()
            for index in range(n_span):
                back_copy(n_span * way + index, base + 1, near - 1).wait_send()
            if direct:
                backy_copy(way, base + 1, near - 1).wait_send()

    went(0)
    hidden_back(0, 0)
    hidden_back(0, 1)

    def ready_grads(block):
        if direct:
            arrivedy(2, block)
        for index in paired:
            arrived(2 + index, block)
        hidden_back(1, block)

    way_back(row_grads, 1, ready_grads)

    def weight_grads(cols):
        for index, target in ((0, gg_ref), (1, gu_ref)):
            total = dot(rx[0, 0, :, cols], dgu[index, 0], contract_first)
            total = total + dot(rx[0, 1, :, cols], dgu[index, 1], contract_first)
            target[cols, :] = total.astype(BF16)
        total = dot(hid[0, 0], rc[0, :, cols], contract_first)
        total = total + dot(hid[0, 1], rc[1, :, cols], contract_first)
        gd_ref[:, cols] = total.astype(BF16)

    def inputs_grad(cols, total):
        ig_ref[:, cols] = total.astype(BF16)

    columns(weight_grads, 0, width, 512)
    weight_grad_copies = [
        pltpu.make_async_copy(source, target, io_sem.at[2 + i])
        for i, (source, target) in enumerate(
            [(gg_ref, gg_hbm), (gu_ref, gu_hbm), (gd_ref, gd_hbm)]
        )
    ]
    for copy in weight_grad_copies:
        copy.start()

    def grad_copy(index):
        cols = half_cols(index)
        return pltpu.make_async_copy(ig_ref.at[:, cols], ig_hbm.at[:, cols], io_sem.at[5 + index])

    give_back(n_span + first, 0)
    give_back(n_span + first, 1)
    if direct:
        send_part(n_span)
    send_part(n_span + first)
    if direct:
        whole(n_span, inputs_grad)
        grad_copy(0).start()
    give_back(n_span + second, 1)
    send_part(n_span + second)
    whole(n_span + first, inputs_grad)
    grad_copy(first).start()
    give_back(n_span + second, 0)

    for step in range(2 + n_span):
        if step != 0:
            raw_copy(step).wait_send()
        for base in (0, near):
            out_copy(step, base + 1, near - 1).wait_send()
            if step in forwarded:
                fwd_copy(step, base, near).wait_send()
    for block in (1, 2, 3):
        meta_copy(block).wait_send()
    for turn in range(2 * n_span):
        part_copy(turn).wait_send()
    if direct:
        for step in range(3):
            for block in (0, 1):
                side_copy(step, block).wait_send()
                outy_copy(step, near * block + 1, near - 1).wait_send()
        for way in (0, 1):
            for block in (0, 1):
                party_copy(way, block).wait_send()
    whole(n_span + second, inputs_grad)
    grad_copy(second).start()
    went(1)
    for index in range(n_span):
        grad_copy(index).wait()
    for copy in weight_grad_copies:
        copy.wait()


def hand_over(pieces, *refs):
    come, leave = refs[12], refs[13]
    given, taken = [], []
    for i in range(4):
        size = refs[i].shape[0] // pieces
        for piece in range(pieces):
            rows = pl.ds(piece * size, size)
            held = refs[8 + i].at[rows]
            given.append(pltpu.make_async_copy(refs[i].at[rows], held, come.at[i, piece]))
            taken.append(pltpu.make_async_copy(held, refs[4 + i].at[rows], leave.at[i, piece]))
    for copy in given:
        copy.start()
    for copy, later in zip(given, taken):
        copy.wait()
        later.start()
    for copy in taken:
        copy.wait()


def shards(
    x_online,
    x_target,
    routes,
    gate_probs,
    expert_place,
    gate_online,
    up_online,
    down_online,
    gate_target,
    up_target,
    down_target,
):
    tok, width = x_online.shape
    slots = expert_place.shape[0]
    n_ex = lax.axis_size("expert")
    cap = 2 * ((2 * tok + slots - 1) // slots)
    rows = slots * cap
    half = gate_online.shape[2]
    paired = 2 * slots == lax.axis_size("dp") * n_ex and n_ex % 2 == 0
    halving = slots & (slots - 1) == 0 and n_ex & (n_ex - 1) == 0
    if cap % 16 or width % 1024 or tok % 128 or slots < 16 or n_ex < 4 or not (paired and halving):
        return shards_plain(
            x_online,
            x_target,
            routes,
            gate_probs,
            expert_place,
            gate_online,
            up_online,
            down_online,
            gate_target,
            up_target,
            down_target,
        )
    direct = 256
    n_span = 3 if direct else 2
    side_cols = max(direct, 128)
    near = slots // 2
    vmem = pl.BlockSpec(memory_space=pltpu.VMEM)
    hbm = pl.BlockSpec(memory_space=pl.ANY)
    dma = pltpu.SemaphoreType.DMA
    outs = pl.pallas_call(
        functools.partial(step_kernel, slots, n_ex, cap, direct),
        out_shape=(
            jax.ShapeDtypeStruct((tok, width), BF16),
            jax.ShapeDtypeStruct((width, half), BF16),
            jax.ShapeDtypeStruct((width, half), BF16),
            jax.ShapeDtypeStruct((half, width), BF16),
        ),
        in_specs=[vmem] * 3 + [hbm] * 8,
        out_specs=(hbm,) * 4,
        scratch_shapes=[
            pltpu.VMEM((tok, width), BF16),
            pltpu.VMEM((tok, width), BF16),
            pltpu.VMEM((tok, width), BF16),
            pltpu.VMEM((width, half), BF16),
            pltpu.VMEM((width, half), BF16),
            pltpu.VMEM((half, width), BF16),
            dma((8,)),
            pltpu.VMEM((2, width, half), BF16),
            pltpu.VMEM((2, width, half), BF16),
            pltpu.VMEM((2, half, width), BF16),
            pltpu.VMEM((3, rows, width), BF16),
            pltpu.VMEM((2, 2, rows, width), BF16),
            pltpu.VMEM((2, rows, width), BF16),
            pltpu.VMEM((2, rows, width), BF16),
            pltpu.VMEM((2, rows, width), BF16),
            pltpu.VMEM((2, rows, width), BF16),
            pltpu.VMEM((2, rows, half), F32),
            pltpu.VMEM((2, rows, half), F32),
            pltpu.VMEM((2, 2, rows, half), BF16),
            pltpu.VMEM((2, 2, rows, half), BF16),
            pltpu.VMEM((4, 8, tok), F32),
            pltpu.VMEM((3, tok, width), BF16),
            pltpu.VMEM((3, tok, width), BF16),
            pltpu.VMEM((2, tok, width), BF16),
            pltpu.VMEM((4, 2, near * cap, tok), BF16),
            pltpu.VMEM((4, 2, tok, near * cap), BF16),
            pltpu.VMEM((3, rows, side_cols), BF16),
            pltpu.VMEM((2, rows, side_cols), BF16),
            pltpu.VMEM((3, 2, tok, side_cols), BF16),
            pltpu.VMEM((2, 2, tok, side_cols), BF16),
            pltpu.VMEM((2, 2, tok, side_cols), BF16),
            dma((6,)),
            dma((2, 3)),
            dma((2, 2 + n_span)),
            dma((2, 2 * n_span)),
            dma((2 + n_span, 2)),
            dma((2 + n_span, slots)),
            dma((2 + n_span, 2)),
            dma((2 + n_span, 2)),
            dma((4, 2)),
            dma((4, slots)),
            dma((2 * n_span, 2)),
            dma((2 * n_span, 2)),
            dma((2, 10)),
            dma((3, 2)),
            dma((3, 2)),
            dma((2, 2)),
            dma((2, 2)),
        ],
        compiler_params=pltpu.CompilerParams(
            collective_id=0, has_side_effects=True, vmem_limit_bytes=60 * 2**20
        ),
    )(
        routes.T,
        gate_probs.T,
        expert_place[None],
        x_online,
        x_target,
        gate_online[0],
        up_online[0],
        down_online[0],
        gate_target[0],
        up_target[0],
        down_target[0],
    )
    pieces = 4
    outs = pl.pallas_call(
        functools.partial(hand_over, pieces),
        out_shape=tuple(jax.ShapeDtypeStruct(o.shape, o.dtype) for o in outs),
        in_specs=[hbm] * 4,
        out_specs=(hbm,) * 4,
        scratch_shapes=[pltpu.VMEM(o.shape, o.dtype) for o in outs]
        + [dma((4, pieces)), dma((4, pieces))],
    )(*outs)
    return (outs[0], outs[1][None], outs[2][None], outs[3][None])


def solution(mesh):
    in_specs = (
        P(("dp", "expert"), None),
        P(("dp", "expert"), None),
        P(("dp", "expert"), None),
        P(("dp", "expert"), None),
        P(),
        P(("dp", "expert"), None, None),
        P(("dp", "expert"), None, None),
        P(("dp", "expert"), None, None),
        P(("dp", "expert"), None, None),
        P(("dp", "expert"), None, None),
        P(("dp", "expert"), None, None),
    )
    out_specs = (
        P(("dp", "expert"), None),
        P(("dp", "expert"), None, None),
        P(("dp", "expert"), None, None),
        P(("dp", "expert"), None, None),
    )
    return jax.shard_map(shards, mesh=mesh, in_specs=in_specs, out_specs=out_specs, check_vma=False)
```

```python
import functools

import jax
import jax.numpy as jnp
from jax import lax
from jax.experimental import pallas as pl
from jax.experimental.pallas import tpu as pltpu
from jax.sharding import PartitionSpec as P

contract_last = (((1,), (1,)), ((), ()))
contract_first = (((0,), (0,)), ((), ()))


def swapped(block, axis, bit):
    count = lax.axis_size(axis)
    route = []
    for low in range(count):
        high = low | 1 << bit
        if high != low and high < count:
            route += [(low, high), (high, low)]
    return lax.ppermute(block, axis, route)


def hidden_forward(inputs, w_gate, w_up):
    pre_gate = jnp.dot(inputs, w_gate, preferred_element_type=jnp.float32)
    pre_up = jnp.dot(inputs, w_up, preferred_element_type=jnp.float32)
    hidden = (jax.nn.silu(pre_gate) * pre_up).astype(jnp.bfloat16)
    return (pre_gate, pre_up, hidden)


def hidden_grads(cotangent, pre_gate, pre_up, w_down):
    d_hidden = lax.dot_general(cotangent, w_down, contract_last, preferred_element_type=jnp.float32)
    sigmoid_gate = jax.nn.sigmoid(pre_gate)
    d_gate = (d_hidden * pre_up * sigmoid_gate * (1.0 + pre_gate * (1.0 - sigmoid_gate))).astype(
        jnp.bfloat16
    )
    d_up = (d_hidden * jax.nn.silu(pre_gate)).astype(jnp.bfloat16)
    return (d_gate, d_up)


def input_rows(d_gate, d_up, w_gate, w_up):
    total = lax.dot_general(d_gate, w_gate, contract_last, preferred_element_type=jnp.float32)
    total = total + lax.dot_general(d_up, w_up, contract_last, preferred_element_type=jnp.float32)
    return total.astype(jnp.bfloat16)


def outer_sum(left, right):
    return lax.dot_general(left, right, contract_first, preferred_element_type=jnp.float32)


def earlier_same(chosen):
    turn = jnp.arange(chosen.shape[0], dtype=jnp.int32)
    alike = (chosen[:, None] == chosen[None, :]) & (turn[None, :] < turn[:, None])
    return jnp.sum(alike.astype(jnp.int32), axis=1)


def shards_plain(
    x_online,
    x_target,
    routes,
    gate_probs,
    expert_place,
    gate_online,
    up_online,
    down_online,
    gate_target,
    up_target,
    down_target,
):
    tok_rows, model_width = x_online.shape
    dp_count = lax.axis_size("dp")
    expert_count = lax.axis_size("expert")
    unit_count = dp_count * expert_count
    experts = expert_place.shape[0]
    capacity = 2 * ((2 * tok_rows + experts - 1) // experts)
    half_cap = capacity // 2
    half_width = gate_online.shape[2]
    chosen = routes.reshape(-1)
    onehot = (chosen[:, None] == jnp.arange(experts, dtype=jnp.int32)[None, :]).astype(jnp.int32)
    position = earlier_same(chosen)
    slot_place = jnp.sum(onehot * expert_place[None, :], axis=1)
    flat_slot = (2 * slot_place + position // half_cap) * half_cap + position % half_cap
    owner_token = jnp.arange(2 * tok_rows, dtype=jnp.int32) // 2

    def to_units(source):
        blank_rows = jnp.zeros((unit_count * half_cap, model_width), source.dtype)
        return (
            blank_rows.at[flat_slot]
            .set(source)
            .reshape(dp_count, expert_count, half_cap, model_width)
        )

    def from_units(block):
        picked = block.reshape(unit_count * half_cap, model_width)[flat_slot]
        return picked.astype(jnp.float32).reshape(tok_rows, 2, model_width)

    partner = swapped(
        (gate_online, up_online, down_online, gate_target, up_target, down_target), "expert", 0
    )
    gate_full = jnp.concatenate([gate_online[0], partner[0][0]], axis=1)
    up_full = jnp.concatenate([up_online[0], partner[1][0]], axis=1)
    down_full = jnp.concatenate([down_online[0], partner[2][0]], axis=0)
    gate_tfull = jnp.concatenate([gate_target[0], partner[3][0]], axis=1)
    up_tfull = jnp.concatenate([up_target[0], partner[4][0]], axis=1)
    down_tfull = jnp.concatenate([down_target[0], partner[5][0]], axis=0)
    recv_online, recv_target = (
        lax.all_to_all(
            lax.all_to_all(
                to_units(x_online[owner_token]), "dp", split_axis=0, concat_axis=0, tiled=True
            ),
            "expert",
            split_axis=1,
            concat_axis=1,
            tiled=True,
        ),
        lax.all_to_all(
            lax.all_to_all(
                to_units(x_target[owner_token]), "dp", split_axis=0, concat_axis=0, tiled=True
            ),
            "expert",
            split_axis=1,
            concat_axis=1,
            tiled=True,
        ),
    )
    unit_shape = recv_online.shape
    inputs_online = recv_online.reshape(-1, model_width)
    inputs_target = recv_target.reshape(-1, model_width)
    pre_gate, pre_up, hidden = hidden_forward(inputs_online, gate_full, up_full)
    out_online = jnp.dot(hidden, down_full, preferred_element_type=jnp.float32).astype(jnp.bfloat16)
    hidden_target = hidden_forward(inputs_target, gate_tfull, up_tfull)[2]
    out_target = jnp.dot(hidden_target, down_tfull, preferred_element_type=jnp.float32).astype(
        jnp.bfloat16
    )
    back_online, back_target = (
        lax.all_to_all(
            lax.all_to_all(
                out_online.reshape(unit_shape), "dp", split_axis=0, concat_axis=0, tiled=True
            ),
            "expert",
            split_axis=1,
            concat_axis=1,
            tiled=True,
        ),
        lax.all_to_all(
            lax.all_to_all(
                out_target.reshape(unit_shape), "dp", split_axis=0, concat_axis=0, tiled=True
            ),
            "expert",
            split_axis=1,
            concat_axis=1,
            tiled=True,
        ),
    )
    y_online = jnp.sum(from_units(back_online) * gate_probs[:, :, None], axis=1)
    y_target = jnp.sum(from_units(back_target) * gate_probs[:, :, None], axis=1)
    cotangent = (
        (gate_probs[:, :, None] * (y_online - y_target)[:, None, :])
        .astype(jnp.bfloat16)
        .reshape(2 * tok_rows, model_width)
    )
    cot_recv = lax.all_to_all(
        lax.all_to_all(to_units(cotangent), "dp", split_axis=0, concat_axis=0, tiled=True),
        "expert",
        split_axis=1,
        concat_axis=1,
        tiled=True,
    )
    cot_rows = cot_recv.reshape(-1, model_width)
    d_gate, d_up = hidden_grads(cot_rows, pre_gate, pre_up, down_full)
    d_rows = input_rows(d_gate, d_up, gate_full, up_full)
    back_grads = lax.all_to_all(
        lax.all_to_all(d_rows.reshape(unit_shape), "dp", split_axis=0, concat_axis=0, tiled=True),
        "expert",
        split_axis=1,
        concat_axis=1,
        tiled=True,
    )
    input_grad = jnp.sum(from_units(back_grads), axis=1).astype(jnp.bfloat16)
    g_gate = outer_sum(inputs_online, d_gate)
    g_up = outer_sum(inputs_online, d_up)
    g_down = outer_sum(hidden, cot_rows)
    sent = (
        swapped(g_gate[:, half_width:].astype(jnp.bfloat16), "expert", 0).astype(jnp.float32),
        swapped(g_up[:, half_width:].astype(jnp.bfloat16), "expert", 0).astype(jnp.float32),
        swapped(g_down[half_width:].astype(jnp.bfloat16), "expert", 0).astype(jnp.float32),
    )
    grad_gate = g_gate[:, :half_width] + sent[0]
    grad_up = g_up[:, :half_width] + sent[1]
    grad_down = g_down[:half_width] + sent[2]
    return (
        input_grad,
        grad_gate.astype(jnp.bfloat16)[None],
        grad_up.astype(jnp.bfloat16)[None],
        grad_down.astype(jnp.bfloat16)[None],
    )


MESH = pl.DeviceIdType.MESH
F32 = jnp.float32
BF16 = jnp.bfloat16


def dot(left, right, dims=(((1,), (0,)), ((), ()))):
    return lax.dot_general(left, right, dims, preferred_element_type=F32)


def step_kernel(
    slots,
    n_ex,
    cap,
    direct,
    routes_ref,
    probs_ref,
    place_ref,
    xo_hbm,
    xt_hbm,
    w0_ref,
    w1_ref,
    w2_ref,
    w3_ref,
    w4_ref,
    w5_ref,
    ig_hbm,
    gg_hbm,
    gu_hbm,
    gd_hbm,
    xo_ref,
    xt_ref,
    ig_ref,
    gg_ref,
    gu_ref,
    gd_ref,
    io_sem,
    wg,
    wu,
    wd,
    sx,
    rx,
    pd,
    pr,
    ret,
    rc,
    pre_g,
    pre_u,
    hid,
    dgu,
    meta,
    raw,
    part_out,
    part_in,
    puts,
    takes,
    sy,
    rety,
    rawy,
    party_out,
    party_in,
    w_sem,
    meta_sem,
    raw_sem,
    part_sem,
    out_send,
    out_recv,
    fwd_send,
    fwd_recv,
    pair_send,
    pair_recv,
    back_send,
    back_recv,
    side_sem,
    outy_send,
    outy_recv,
    backy_send,
    backy_recv,
):
    tok, width = xo_ref.shape
    near = slots // 2
    half_rows = near * cap
    dp, ex = lax.axis_index("dp"), lax.axis_index("expert")
    side = lax.rem(ex, 2)
    planes = n_ex // 2
    group = slots // planes
    z = lax.div(ex, 2)
    z_far = lax.rem(z + planes // 2, planes)
    me = dp * planes + z
    me_far = dp * planes + z_far
    partner = (dp, 2 * z + 1 - side)
    twin = (dp, 2 * z_far + side)
    cross = (dp, 2 * z_far + 1 - side)

    middle = direct + (width - direct) // 512 * 256
    spans = ([(0, direct)] if direct else []) + [(direct, middle), (middle, width)]
    paired = [i for i, span in enumerate(spans) if span[0] >= direct]
    n_span = len(spans)
    first, second = paired

    def other(i):
        mask = lax.rem(i, group) * planes + lax.div(i, group)
        slot, power = 0, 1
        while power < slots:
            bit = lax.rem(lax.rem(lax.div(me, power), 2) + lax.rem(lax.div(mask, power), 2), 2)
            slot, power = slot + bit * power, 2 * power
        return slot

    def peer(o):
        unit = 2 * other(lax.rem(o, near)) + side
        return (lax.div(unit, n_ex), lax.rem(unit, n_ex))

    def chunk(index, many=1):
        return pl.ds(pl.multiple_of(index * cap, cap), many * cap)

    def each(low, high, body):
        def step(o, carry):
            body(o)
            return carry

        lax.fori_loop(low, high, step, 0)

    def each_down(low, high, body):
        each(0, high - low, lambda o: body(high - 1 - o))

    def columns(body, low=0, high=width, tile=256):
        each(
            low // tile, high // tile, lambda i: body(pl.ds(pl.multiple_of(i * tile, tile), tile))
        )

    def strips(body, low=0, high=width, tile=512):
        for start in range(low, high, tile):
            body(pl.ds(start, min(tile, high - start)))

    def remote(source, target, send, recv, device):
        return pltpu.make_async_remote_copy(
            src_ref=source,
            dst_ref=target,
            send_sem=send,
            recv_sem=recv,
            device_id=device,
            device_id_type=MESH,
        )

    input_copies = [
        pltpu.make_async_copy(xo_hbm, xo_ref, io_sem.at[0]),
        pltpu.make_async_copy(xt_hbm, xt_ref, io_sem.at[1]),
    ]
    for copy in input_copies:
        copy.start()

    barrier = pltpu.get_barrier_semaphore()
    each(
        1,
        near,
        lambda o: pl.semaphore_signal(barrier, inc=1, device_id=peer(o), device_id_type=MESH),
    )
    for device in (partner, twin, cross):
        pl.semaphore_signal(barrier, inc=1, device_id=device, device_id_type=MESH)

    weight_copies = [
        pltpu.make_async_copy(source, target, w_sem.at[i])
        for i, (source, target) in enumerate(
            [
                (w0_ref, wg.at[0]),
                (w1_ref, wu.at[0]),
                (w2_ref, wd.at[0]),
                (w3_ref, wg.at[1]),
                (w4_ref, wu.at[1]),
                (w5_ref, wd.at[1]),
            ]
        )
    ]
    for copy in weight_copies:
        copy.start()

    def one_hot(compare):
        return jnp.where(compare, 1.0, 0.0).astype(BF16)

    def stand(line):
        size = line.shape[1]
        here = [lax.broadcasted_iota(jnp.int32, (size, size), d) for d in range(2)]
        return jnp.sum(jnp.where(here[0] == here[1], line, 0.0), axis=1, keepdims=True)

    def count(mask, axis):
        return jnp.sum(jnp.where(mask, 1.0, 0.0), axis=axis, keepdims=True)

    meta[0, 0:2, :] = routes_ref[...].astype(F32)
    meta[0, 2:4, :] = probs_ref[...]
    meta[0, 4:8, :] = jnp.zeros((4, tok), F32)

    def meta_copy(block):
        device = (twin, partner, cross)[block - 1]
        sem = meta_sem.at[0, block - 1], meta_sem.at[1, block - 1]
        return remote(meta.at[0], meta.at[block], *sem, device)

    def order_of(slot, home):
        mask = slot.astype(jnp.int32) ^ home
        return lax.rem(mask, planes) * group + lax.div(mask, planes)

    def tables(block):
        home = me_far if block % 2 else me
        low = half_rows * (block % 2)
        down, across = [lax.broadcasted_iota(jnp.int32, (tok, tok), d) for d in range(2)]
        line = [meta[block, k : k + 1, :] for k in range(2)]
        tall = [stand(line[k]) for k in range(2)]
        place = place_ref[...].astype(F32)
        place_tall = stand(place)
        ids_line = lax.broadcasted_iota(jnp.int32, (tok, slots), 1).astype(F32)
        ids_tall = lax.broadcasted_iota(jnp.int32, (slots, tok), 0).astype(F32)
        row_iota = lax.broadcasted_iota(jnp.int32, (half_rows, tok), 0) + low
        col_iota = lax.broadcasted_iota(jnp.int32, (tok, half_rows), 1) + low
        for k in range(2):
            alike = (line[k] == tall[0]) | (line[k] == tall[1])
            slot = jnp.sum(jnp.where(ids_tall == line[k], place_tall, 0.0), axis=0, keepdims=True)
            before = count(alike & (down < across), 0).astype(jnp.int32)
            puts[block, k] = one_hot(row_iota == order_of(slot, home) * cap + before)
            alike = (tall[k] == line[0]) | (tall[k] == line[1])
            slot = jnp.sum(jnp.where(ids_line == tall[k], place, 0.0), axis=1, keepdims=True)
            before = count(alike & (across < down), 1).astype(jnp.int32)
            takes[block, k] = one_hot(col_iota == order_of(slot, home) * cap + before)

    def probs_of(block):
        return [stand(meta[block, 2 + k : 3 + k, :]) for k in range(2)]

    def rows_of(block):
        return pl.ds(half_rows * (block % 2), half_rows)

    def place_rows(target, block, source, low, high):
        put = puts[block, 0] + puts[block, 1]

        def body(cols):
            target[rows_of(block), cols] = dot(put, source[:, cols]).astype(BF16)

        strips(body, low, high)

    def span_of(step):
        return (0, width) if step < 2 else spans[step - 2]

    def into(step):
        return rx.at[step] if step < 2 else rc

    def out_copy(step, o, many=1):
        low, high = span_of(step)
        cols = pl.ds(low, high - low)
        return remote(
            sx.at[min(step, 2), chunk(o, many), cols],
            into(step).at[0, chunk(o, many), cols],
            out_send.at[step, lax.div(o, near)],
            out_recv.at[step, o],
            peer(o),
        )

    def fwd_copy(step, o, many=1):
        low, high = span_of(step)
        low = max(low, direct)
        here = into(step)
        cols = pl.ds(low, high - low)
        return remote(
            here.at[0, chunk(o, many), cols],
            here.at[1, chunk(o, many), cols],
            fwd_send.at[step, lax.div(o, near)],
            fwd_recv.at[step, lax.div(o, near)],
            partner,
        )

    forwarded = [0, 1] + [2 + i for i in paired]

    def begin(step, block):
        base = near * block
        each(base + 1, base + near, lambda o: out_copy(step, o).start())
        low, high = span_of(step)
        cols = pl.ds(low, high - low)
        into(step)[0, pl.ds(base * cap, cap), cols] = sx[min(step, 2), pl.ds(base * cap, cap), cols]
        if step in forwarded:
            fwd_copy(step, base).start()

    def relay(step, low, high):
        def body(o):
            out_copy(step, o).wait_recv()
            if step in forwarded:
                fwd_copy(step, o).start()

        each(low, high, body)

    def arrived(step, block):
        fwd_copy(step, near * block, near).wait_recv()

    def outy_copy(step, o, many=1):
        target = rx.at[step] if step < 2 else rc
        return remote(
            sy.at[step, chunk(o, many)],
            target.at[1, chunk(o, many), pl.ds(0, direct)],
            outy_send.at[step, lax.div(o, near)],
            outy_recv.at[step, lax.div(o, near)],
            peer(o),
        )

    def beginy(step, block):
        base = near * block
        each(base + 1, base + near, lambda o: outy_copy(step, o).start())
        target = rx.at[step] if step < 2 else rc
        target[1, pl.ds(base * cap, cap), 0:direct] = sy[step, pl.ds(base * cap, cap)]

    def arrivedy(step, block):
        outy_copy(step, near * block + 1, near - 1).wait_recv()

    def raw_copy(step):
        low, high = span_of(step)
        cols = pl.ds(low, high - low)
        source = (xo_ref, xt_ref)[step] if step < 2 else part_out.at[2]
        return remote(
            source.at[:, cols],
            raw.at[min(step, 2), :, cols],
            raw_sem.at[0, step],
            raw_sem.at[1, step],
            twin,
        )

    def side_copy(step, block):
        cols = pl.ds(0, direct)
        source = (xo_ref, xt_ref, part_out.at[2])[step] if block == 0 else raw.at[step]
        return remote(
            source.at[:, cols],
            rawy.at[step, block],
            side_sem.at[0, 2 * step + block],
            side_sem.at[1, 2 * step + block],
            partner,
        )

    def half_cols(turn):
        low, high = spans[turn % n_span]
        return pl.ds(low, high - low)

    def paired_turn(turn):
        return 2 * (turn // n_span) + paired.index(turn % n_span)

    def pair_copy(turn, o, many=1):
        return remote(
            pd.at[1, chunk(o, many), half_cols(turn)],
            pr.at[turn // n_span, chunk(o, many), half_cols(turn)],
            pair_send.at[paired_turn(turn), lax.div(o, near)],
            pair_recv.at[paired_turn(turn), o],
            partner,
        )

    def back_copy(turn, o, many=1):
        return remote(
            pd.at[0, chunk(o, many), half_cols(turn)],
            ret.at[turn // n_span, chunk(o, many), half_cols(turn)],
            back_send.at[turn, lax.div(o, near)],
            back_recv.at[turn, lax.div(o, near)],
            peer(o),
        )

    def backy_copy(way, o, many=1):
        return remote(
            pd.at[1, chunk(o, many), pl.ds(0, direct)],
            rety.at[way, chunk(o, many)],
            backy_send.at[way, lax.div(o, near)],
            backy_recv.at[way, lax.div(o, near)],
            peer(o),
        )

    def add_part(turn, o):
        pair_copy(turn, o).wait_recv()
        cols = half_cols(turn)
        total = pd[0, chunk(o), cols].astype(F32) + pr[turn // n_span, chunk(o), cols].astype(F32)
        return total.astype(BF16)

    def give_back(turn, block):
        base = near * block

        def body(o):
            pd[0, chunk(o), half_cols(turn)] = add_part(turn, o)
            back_copy(turn, o).start()

        each_down(base + 1, base + near, body)
        ret[turn // n_span, pl.ds(base * cap, cap), half_cols(turn)] = add_part(turn, base)

    def give_direct(way, block):
        base, turn = near * block, n_span * way

        def body(o):
            back_copy(turn, o).start()
            backy_copy(way, o).start()

        each_down(base + 1, base + near, body)
        own = pl.ds(base * cap, cap)
        ret[way, own, 0:direct] = pd[0, own, 0:direct]
        rety[way, own] = pd[1, own, 0:direct]

    def back_came(turn, block):
        back_copy(turn, near * block + 1, near - 1).wait_recv()

    def backy_came(way, block):
        backy_copy(way, near * block + 1, near - 1).wait_recv()

    def part_copy(turn):
        way, cols = turn // n_span, half_cols(turn)
        return remote(
            part_out.at[way, :, cols],
            part_in.at[way, :, cols],
            part_sem.at[0, turn],
            part_sem.at[1, turn],
            twin,
        )

    def party_copy(way, block):
        return remote(
            party_out.at[way, block],
            party_in.at[way, block],
            side_sem.at[0, 6 + 2 * way + block],
            side_sem.at[1, 6 + 2 * way + block],
            partner,
        )

    def picked(way, block, source):
        if way == 0:
            p0, p1 = probs_of(block)
            return p0 * dot(takes[block, 0], source) + p1 * dot(takes[block, 1], source)
        return dot(takes[block, 0] + takes[block, 1], source)

    def send_side(way, block):
        backy_came(way, block)
        rows = rows_of(block)

        def body(cols):
            party_out[way, block, :, cols] = picked(way, 2 + block, rety[way, rows, cols]).astype(
                BF16
            )

        strips(body, 0, direct)
        party_copy(way, block).start()

    def send_part(turn):
        way = turn // n_span
        straight = spans[turn % n_span][0] < direct
        back_came(turn, 1)
        if straight:
            party_copy(way, 1).wait_recv()

        def body(cols):
            total = picked(way, 1, ret[way, rows_of(1), cols])
            if straight:
                total = total + party_in[way, 1, :, cols].astype(F32)
            part_out[way, :, cols] = total.astype(BF16)

        strips(body, *spans[turn % n_span])
        part_copy(turn).start()

    def whole(turn, use):
        way = turn // n_span
        straight = spans[turn % n_span][0] < direct
        back_came(turn, 0)
        if straight:
            party_copy(way, 0).wait_recv()
        part_copy(turn).wait_recv()

        def body(cols):
            total = picked(way, 0, ret[way, rows_of(0), cols])
            total = total + part_in[way, :, cols].astype(F32)
            if straight:
                total = total + party_in[way, 0, :, cols].astype(F32)
            use(cols, total)

        strips(body, *spans[turn % n_span])

    def cotangents(block, diff):
        p0, p1 = probs_of(block)
        rows0, rows1 = (p0 * diff).astype(BF16), (p1 * diff).astype(BF16)
        return (dot(puts[block, 0], rows0) + dot(puts[block, 1], rows1)).astype(BF16)

    def own_cotangents(index):
        def use(cols, diff):
            part_out[2, :, cols] = diff.astype(BF16)
            sx[2, rows_of(0), cols] = cotangents(0, diff)

        whole(index, use)
        raw_copy(2 + index).start()
        if spans[index][0] < direct:
            side_copy(2, 0).start()
        begin(2 + index, 0)

    def twin_cotangents(index):
        raw_copy(2 + index).wait_recv()
        if spans[index][0] < direct:
            side_copy(2, 1).start()

        def body(cols):
            sx[2, rows_of(1), cols] = cotangents(1, raw[2, :, cols].astype(F32))

        strips(body, *spans[index])
        begin(2 + index, 1)

    def side_cotangents(block):
        side_copy(2, block).wait_recv()

        def body(cols):
            sy[2, rows_of(block), cols] = cotangents(2 + block, rawy[2, block, :, cols].astype(F32))

        strips(body, 0, direct)
        beginy(2, block)

    def side_inputs(net, block):
        side_copy(net, block).wait_recv()
        place_rows(sy.at[net], 2 + block, rawy.at[net, block], 0, direct)
        beginy(net, block)

    def forward(net, part, block):
        rows = rows_of(block)
        gate = dot(rx[net, part, rows], wg[net])
        up = dot(rx[net, part, rows], wu[net])
        hid[net, part, rows] = (gate * jax.nn.sigmoid(gate) * up).astype(BF16)
        if net == 0:
            pre_g[part, rows] = gate
            pre_u[part, rows] = up

    tables(0)
    input_copies[0].wait()
    place_rows(sx.at[0], 0, xo_ref, 0, width)
    pl.semaphore_wait(barrier, near + 2)
    for block in (1, 2, 3):
        meta_copy(block).start()
    raw_copy(0).start()
    begin(0, 0)
    if direct:
        side_copy(0, 0).start()
    input_copies[1].wait()
    place_rows(sx.at[1], 0, xt_ref, 0, width)
    begin(1, 0)
    if direct:
        side_copy(1, 0).start()
    relay(0, 1, near // 2)
    for block in (2, 1, 3):
        meta_copy(block).wait_recv()
    if direct:
        tables(2)
        side_inputs(0, 0)
    relay(0, near // 2, near)
    tables(1)
    if direct:
        side_inputs(1, 0)
    relay(1, 1, near // 2)
    raw_copy(0).wait_recv()
    raw_copy(0).wait_send()
    raw_copy(1).start()
    place_rows(sx.at[0], 1, raw.at[0], 0, width)
    begin(0, 1)
    if direct:
        side_copy(0, 1).start()
        tables(3)
    relay(1, near // 2, near)
    for copy in weight_copies:
        copy.wait()
    forward(0, 0, 0)
    relay(0, near + 1, slots)
    if direct:
        side_inputs(0, 1)
    raw_copy(1).wait_recv()
    place_rows(sx.at[1], 1, raw.at[1], 0, width)
    begin(1, 1)
    if direct:
        side_copy(1, 1).start()

    def landed(step, block):
        arrived(step, block)
        if direct and step < 2:
            arrivedy(step, block)

    forward(1, 0, 0)
    forward(0, 0, 1)
    landed(0, 0)
    forward(0, 1, 0)
    relay(1, near + 1, slots)
    if direct:
        side_inputs(1, 1)
    forward(1, 0, 1)
    landed(0, 1)
    forward(0, 1, 1)

    def outputs(index, part, block):
        rows = rows_of(block)

        def body(cols):
            diff = dot(hid[0, part, rows], wd[0, :, cols]) - dot(hid[1, part, rows], wd[1, :, cols])
            pd[part, rows, cols] = diff.astype(BF16)

        strips(body, *spans[index])

    def row_grads(index, part, block):
        rows = rows_of(block)

        def body(cols):
            total = dot(dgu[0, part, rows], wg[0, cols, :], contract_last)
            total = total + dot(dgu[1, part, rows], wu[0, cols, :], contract_last)
            pd[part, rows, cols] = total.astype(BF16)

        strips(body, *spans[index])

    def exchange(rows_out, way, block, index):
        rows_out(index, 1, block)
        turn = n_span * way + index
        each_down(near * block, near * block + near, lambda o: pair_copy(turn, o).start())

    def way_back(rows_out, way, ready):
        for block in (0, 1):
            ready(block)
            if direct:
                for part in (0, 1):
                    rows_out(0, part, block)
                give_direct(way, block)
            exchange(rows_out, way, block, first)
        for block in (0, 1):
            rows_out(first, 0, block)
        if direct:
            send_side(way, 1)
            send_side(way, 0)
        for block in (1, 0):
            exchange(rows_out, way, block, second)
        for block in (1, 0):
            rows_out(second, 0, block)

    def ready_outputs(block):
        landed(1, block)
        forward(1, 1, block)

    way_back(outputs, 0, ready_outputs)
    give_back(first, 0)
    give_back(first, 1)
    if direct:
        send_part(0)
    send_part(first)
    if direct:
        own_cotangents(0)
    give_back(second, 1)
    own_cotangents(first)
    if direct:
        twin_cotangents(0)
    send_part(second)
    give_back(second, 0)
    relay(2 + first, 1, near)
    twin_cotangents(first)
    own_cotangents(second)
    if direct:
        side_cotangents(0)
    relay(2 + first, near + 1, slots)
    relay(2 + second, 1, near)
    if direct:
        side_cotangents(1)
    twin_cotangents(second)
    relay(2 + second, near + 1, slots)
    if direct:
        relay(2, 1, near)
        relay(2, near + 1, slots)

    def hidden_back(part, block):
        rows = rows_of(block)
        d_hidden = dot(rc[part, rows], wd[0], contract_last)
        gate, up = pre_g[part, rows], pre_u[part, rows]
        sig = jax.nn.sigmoid(gate)
        dgu[0, part, rows] = (d_hidden * up * sig * (1.0 + gate * (1.0 - sig))).astype(BF16)
        dgu[1, part, rows] = (d_hidden * (gate * sig)).astype(BF16)

    def went(way):
        for base in (0, near):
            for index in paired:
                pair_copy(n_span * way + index, base, near).wait_send()
            for index in range(n_span):
                back_copy(n_span * way + index, base + 1, near - 1).wait_send()
            if direct:
                backy_copy(way, base + 1, near - 1).wait_send()

    went(0)
    hidden_back(0, 0)
    hidden_back(0, 1)

    def ready_grads(block):
        if direct:
            arrivedy(2, block)
        for index in paired:
            arrived(2 + index, block)
        hidden_back(1, block)

    way_back(row_grads, 1, ready_grads)

    def weight_grads(cols):
        for index, target in ((0, gg_ref), (1, gu_ref)):
            total = dot(rx[0, 0, :, cols], dgu[index, 0], contract_first)
            total = total + dot(rx[0, 1, :, cols], dgu[index, 1], contract_first)
            target[cols, :] = total.astype(BF16)
        total = dot(hid[0, 0], rc[0, :, cols], contract_first)
        total = total + dot(hid[0, 1], rc[1, :, cols], contract_first)
        gd_ref[:, cols] = total.astype(BF16)

    def inputs_grad(cols, total):
        ig_ref[:, cols] = total.astype(BF16)

    columns(weight_grads, 0, width, 512)
    weight_grad_copies = [
        pltpu.make_async_copy(source, target, io_sem.at[2 + i])
        for i, (source, target) in enumerate(
            [(gg_ref, gg_hbm), (gu_ref, gu_hbm), (gd_ref, gd_hbm)]
        )
    ]
    for copy in weight_grad_copies:
        copy.start()

    def grad_copy(index):
        cols = half_cols(index)
        return pltpu.make_async_copy(ig_ref.at[:, cols], ig_hbm.at[:, cols], io_sem.at[5 + index])

    give_back(n_span + first, 0)
    give_back(n_span + first, 1)
    if direct:
        send_part(n_span)
    send_part(n_span + first)
    if direct:
        whole(n_span, inputs_grad)
        grad_copy(0).start()
    give_back(n_span + second, 1)
    send_part(n_span + second)
    whole(n_span + first, inputs_grad)
    grad_copy(first).start()
    give_back(n_span + second, 0)

    for step in range(2 + n_span):
        if step != 0:
            raw_copy(step).wait_send()
        for base in (0, near):
            out_copy(step, base + 1, near - 1).wait_send()
            if step in forwarded:
                fwd_copy(step, base, near).wait_send()
    for block in (1, 2, 3):
        meta_copy(block).wait_send()
    for turn in range(2 * n_span):
        part_copy(turn).wait_send()
    if direct:
        for step in range(3):
            for block in (0, 1):
                side_copy(step, block).wait_send()
                outy_copy(step, near * block + 1, near - 1).wait_send()
        for way in (0, 1):
            for block in (0, 1):
                party_copy(way, block).wait_send()
    whole(n_span + second, inputs_grad)
    grad_copy(second).start()
    went(1)
    for index in range(n_span):
        grad_copy(index).wait()
    for copy in weight_grad_copies:
        copy.wait()


def hand_over(pieces, *refs):
    come, leave = refs[12], refs[13]
    given, taken = [], []
    for i in range(4):
        size = refs[i].shape[0] // pieces
        for piece in range(pieces):
            rows = pl.ds(piece * size, size)
            held = refs[8 + i].at[rows]
            given.append(pltpu.make_async_copy(refs[i].at[rows], held, come.at[i, piece]))
            taken.append(pltpu.make_async_copy(held, refs[4 + i].at[rows], leave.at[i, piece]))
    for copy in given:
        copy.start()
    for copy, later in zip(given, taken):
        copy.wait()
        later.start()
    for copy in taken:
        copy.wait()


def shards(
    x_online,
    x_target,
    routes,
    gate_probs,
    expert_place,
    gate_online,
    up_online,
    down_online,
    gate_target,
    up_target,
    down_target,
):
    tok, width = x_online.shape
    slots = expert_place.shape[0]
    n_ex = lax.axis_size("expert")
    cap = 2 * ((2 * tok + slots - 1) // slots)
    rows = slots * cap
    half = gate_online.shape[2]
    paired = 2 * slots == lax.axis_size("dp") * n_ex and n_ex % 2 == 0
    halving = slots & (slots - 1) == 0 and n_ex & (n_ex - 1) == 0
    if cap % 16 or width % 1024 or tok % 128 or slots < 16 or n_ex < 4 or not (paired and halving):
        return shards_plain(
            x_online,
            x_target,
            routes,
            gate_probs,
            expert_place,
            gate_online,
            up_online,
            down_online,
            gate_target,
            up_target,
            down_target,
        )
    direct = 256
    n_span = 3 if direct else 2
    side_cols = max(direct, 128)
    near = slots // 2
    vmem = pl.BlockSpec(memory_space=pltpu.VMEM)
    hbm = pl.BlockSpec(memory_space=pl.ANY)
    dma = pltpu.SemaphoreType.DMA
    outs = pl.pallas_call(
        functools.partial(step_kernel, slots, n_ex, cap, direct),
        out_shape=(
            jax.ShapeDtypeStruct((tok, width), BF16),
            jax.ShapeDtypeStruct((width, half), BF16),
            jax.ShapeDtypeStruct((width, half), BF16),
            jax.ShapeDtypeStruct((half, width), BF16),
        ),
        in_specs=[vmem] * 3 + [hbm] * 8,
        out_specs=(hbm,) * 4,
        scratch_shapes=[
            pltpu.VMEM((tok, width), BF16),
            pltpu.VMEM((tok, width), BF16),
            pltpu.VMEM((tok, width), BF16),
            pltpu.VMEM((width, half), BF16),
            pltpu.VMEM((width, half), BF16),
            pltpu.VMEM((half, width), BF16),
            dma((8,)),
            pltpu.VMEM((2, width, half), BF16),
            pltpu.VMEM((2, width, half), BF16),
            pltpu.VMEM((2, half, width), BF16),
            pltpu.VMEM((3, rows, width), BF16),
            pltpu.VMEM((2, 2, rows, width), BF16),
            pltpu.VMEM((2, rows, width), BF16),
            pltpu.VMEM((2, rows, width), BF16),
            pltpu.VMEM((2, rows, width), BF16),
            pltpu.VMEM((2, rows, width), BF16),
            pltpu.VMEM((2, rows, half), F32),
            pltpu.VMEM((2, rows, half), F32),
            pltpu.VMEM((2, 2, rows, half), BF16),
            pltpu.VMEM((2, 2, rows, half), BF16),
            pltpu.VMEM((4, 8, tok), F32),
            pltpu.VMEM((3, tok, width), BF16),
            pltpu.VMEM((3, tok, width), BF16),
            pltpu.VMEM((2, tok, width), BF16),
            pltpu.VMEM((4, 2, near * cap, tok), BF16),
            pltpu.VMEM((4, 2, tok, near * cap), BF16),
            pltpu.VMEM((3, rows, side_cols), BF16),
            pltpu.VMEM((2, rows, side_cols), BF16),
            pltpu.VMEM((3, 2, tok, side_cols), BF16),
            pltpu.VMEM((2, 2, tok, side_cols), BF16),
            pltpu.VMEM((2, 2, tok, side_cols), BF16),
            dma((6,)),
            dma((2, 3)),
            dma((2, 2 + n_span)),
            dma((2, 2 * n_span)),
            dma((2 + n_span, 2)),
            dma((2 + n_span, slots)),
            dma((2 + n_span, 2)),
            dma((2 + n_span, 2)),
            dma((4, 2)),
            dma((4, slots)),
            dma((2 * n_span, 2)),
            dma((2 * n_span, 2)),
            dma((2, 10)),
            dma((3, 2)),
            dma((3, 2)),
            dma((2, 2)),
            dma((2, 2)),
        ],
        compiler_params=pltpu.CompilerParams(
            collective_id=0, has_side_effects=True, vmem_limit_bytes=60 * 2**20
        ),
    )(
        routes.T,
        gate_probs.T,
        expert_place[None],
        x_online,
        x_target,
        gate_online[0],
        up_online[0],
        down_online[0],
        gate_target[0],
        up_target[0],
        down_target[0],
    )
    pieces = 2
    outs = pl.pallas_call(
        functools.partial(hand_over, pieces),
        out_shape=tuple(jax.ShapeDtypeStruct(o.shape, o.dtype) for o in outs),
        in_specs=[hbm] * 4,
        out_specs=(hbm,) * 4,
        scratch_shapes=[pltpu.VMEM(o.shape, o.dtype) for o in outs]
        + [dma((4, pieces)), dma((4, pieces))],
    )(*outs)
    return (outs[0], outs[1][None], outs[2][None], outs[3][None])


def solution(mesh):
    in_specs = (
        P(("dp", "expert"), None),
        P(("dp", "expert"), None),
        P(("dp", "expert"), None),
        P(("dp", "expert"), None),
        P(),
        P(("dp", "expert"), None, None),
        P(("dp", "expert"), None, None),
        P(("dp", "expert"), None, None),
        P(("dp", "expert"), None, None),
        P(("dp", "expert"), None, None),
        P(("dp", "expert"), None, None),
    )
    out_specs = (
        P(("dp", "expert"), None),
        P(("dp", "expert"), None, None),
        P(("dp", "expert"), None, None),
        P(("dp", "expert"), None, None),
    )
    return jax.shard_map(shards, mesh=mesh, in_specs=in_specs, out_specs=out_specs, check_vma=False)
```

```python
import functools

import jax
import jax.numpy as jnp
from jax import lax
from jax.experimental import pallas as pl
from jax.experimental.pallas import tpu as pltpu
from jax.sharding import PartitionSpec as P

contract_last = (((1,), (1,)), ((), ()))
contract_first = (((0,), (0,)), ((), ()))


def swapped(block, axis, bit):
    count = lax.axis_size(axis)
    route = []
    for low in range(count):
        high = low | 1 << bit
        if high != low and high < count:
            route += [(low, high), (high, low)]
    return lax.ppermute(block, axis, route)


def hidden_forward(inputs, w_gate, w_up):
    pre_gate = jnp.dot(inputs, w_gate, preferred_element_type=jnp.float32)
    pre_up = jnp.dot(inputs, w_up, preferred_element_type=jnp.float32)
    hidden = (jax.nn.silu(pre_gate) * pre_up).astype(jnp.bfloat16)
    return (pre_gate, pre_up, hidden)


def hidden_grads(cotangent, pre_gate, pre_up, w_down):
    d_hidden = lax.dot_general(cotangent, w_down, contract_last, preferred_element_type=jnp.float32)
    sigmoid_gate = jax.nn.sigmoid(pre_gate)
    d_gate = (d_hidden * pre_up * sigmoid_gate * (1.0 + pre_gate * (1.0 - sigmoid_gate))).astype(
        jnp.bfloat16
    )
    d_up = (d_hidden * jax.nn.silu(pre_gate)).astype(jnp.bfloat16)
    return (d_gate, d_up)


def input_rows(d_gate, d_up, w_gate, w_up):
    total = lax.dot_general(d_gate, w_gate, contract_last, preferred_element_type=jnp.float32)
    total = total + lax.dot_general(d_up, w_up, contract_last, preferred_element_type=jnp.float32)
    return total.astype(jnp.bfloat16)


def outer_sum(left, right):
    return lax.dot_general(left, right, contract_first, preferred_element_type=jnp.float32)


def earlier_same(chosen):
    turn = jnp.arange(chosen.shape[0], dtype=jnp.int32)
    alike = (chosen[:, None] == chosen[None, :]) & (turn[None, :] < turn[:, None])
    return jnp.sum(alike.astype(jnp.int32), axis=1)


def shards_plain(
    x_online,
    x_target,
    routes,
    gate_probs,
    expert_place,
    gate_online,
    up_online,
    down_online,
    gate_target,
    up_target,
    down_target,
):
    tok_rows, model_width = x_online.shape
    dp_count = lax.axis_size("dp")
    expert_count = lax.axis_size("expert")
    unit_count = dp_count * expert_count
    experts = expert_place.shape[0]
    capacity = 2 * ((2 * tok_rows + experts - 1) // experts)
    half_cap = capacity // 2
    half_width = gate_online.shape[2]
    chosen = routes.reshape(-1)
    onehot = (chosen[:, None] == jnp.arange(experts, dtype=jnp.int32)[None, :]).astype(jnp.int32)
    position = earlier_same(chosen)
    slot_place = jnp.sum(onehot * expert_place[None, :], axis=1)
    flat_slot = (2 * slot_place + position // half_cap) * half_cap + position % half_cap
    owner_token = jnp.arange(2 * tok_rows, dtype=jnp.int32) // 2

    def to_units(source):
        blank_rows = jnp.zeros((unit_count * half_cap, model_width), source.dtype)
        return (
            blank_rows.at[flat_slot]
            .set(source)
            .reshape(dp_count, expert_count, half_cap, model_width)
        )

    def from_units(block):
        picked = block.reshape(unit_count * half_cap, model_width)[flat_slot]
        return picked.astype(jnp.float32).reshape(tok_rows, 2, model_width)

    partner = swapped(
        (gate_online, up_online, down_online, gate_target, up_target, down_target), "expert", 0
    )
    gate_full = jnp.concatenate([gate_online[0], partner[0][0]], axis=1)
    up_full = jnp.concatenate([up_online[0], partner[1][0]], axis=1)
    down_full = jnp.concatenate([down_online[0], partner[2][0]], axis=0)
    gate_tfull = jnp.concatenate([gate_target[0], partner[3][0]], axis=1)
    up_tfull = jnp.concatenate([up_target[0], partner[4][0]], axis=1)
    down_tfull = jnp.concatenate([down_target[0], partner[5][0]], axis=0)
    recv_online, recv_target = (
        lax.all_to_all(
            lax.all_to_all(
                to_units(x_online[owner_token]), "dp", split_axis=0, concat_axis=0, tiled=True
            ),
            "expert",
            split_axis=1,
            concat_axis=1,
            tiled=True,
        ),
        lax.all_to_all(
            lax.all_to_all(
                to_units(x_target[owner_token]), "dp", split_axis=0, concat_axis=0, tiled=True
            ),
            "expert",
            split_axis=1,
            concat_axis=1,
            tiled=True,
        ),
    )
    unit_shape = recv_online.shape
    inputs_online = recv_online.reshape(-1, model_width)
    inputs_target = recv_target.reshape(-1, model_width)
    pre_gate, pre_up, hidden = hidden_forward(inputs_online, gate_full, up_full)
    out_online = jnp.dot(hidden, down_full, preferred_element_type=jnp.float32).astype(jnp.bfloat16)
    hidden_target = hidden_forward(inputs_target, gate_tfull, up_tfull)[2]
    out_target = jnp.dot(hidden_target, down_tfull, preferred_element_type=jnp.float32).astype(
        jnp.bfloat16
    )
    back_online, back_target = (
        lax.all_to_all(
            lax.all_to_all(
                out_online.reshape(unit_shape), "dp", split_axis=0, concat_axis=0, tiled=True
            ),
            "expert",
            split_axis=1,
            concat_axis=1,
            tiled=True,
        ),
        lax.all_to_all(
            lax.all_to_all(
                out_target.reshape(unit_shape), "dp", split_axis=0, concat_axis=0, tiled=True
            ),
            "expert",
            split_axis=1,
            concat_axis=1,
            tiled=True,
        ),
    )
    y_online = jnp.sum(from_units(back_online) * gate_probs[:, :, None], axis=1)
    y_target = jnp.sum(from_units(back_target) * gate_probs[:, :, None], axis=1)
    cotangent = (
        (gate_probs[:, :, None] * (y_online - y_target)[:, None, :])
        .astype(jnp.bfloat16)
        .reshape(2 * tok_rows, model_width)
    )
    cot_recv = lax.all_to_all(
        lax.all_to_all(to_units(cotangent), "dp", split_axis=0, concat_axis=0, tiled=True),
        "expert",
        split_axis=1,
        concat_axis=1,
        tiled=True,
    )
    cot_rows = cot_recv.reshape(-1, model_width)
    d_gate, d_up = hidden_grads(cot_rows, pre_gate, pre_up, down_full)
    d_rows = input_rows(d_gate, d_up, gate_full, up_full)
    back_grads = lax.all_to_all(
        lax.all_to_all(d_rows.reshape(unit_shape), "dp", split_axis=0, concat_axis=0, tiled=True),
        "expert",
        split_axis=1,
        concat_axis=1,
        tiled=True,
    )
    input_grad = jnp.sum(from_units(back_grads), axis=1).astype(jnp.bfloat16)
    g_gate = outer_sum(inputs_online, d_gate)
    g_up = outer_sum(inputs_online, d_up)
    g_down = outer_sum(hidden, cot_rows)
    sent = (
        swapped(g_gate[:, half_width:].astype(jnp.bfloat16), "expert", 0).astype(jnp.float32),
        swapped(g_up[:, half_width:].astype(jnp.bfloat16), "expert", 0).astype(jnp.float32),
        swapped(g_down[half_width:].astype(jnp.bfloat16), "expert", 0).astype(jnp.float32),
    )
    grad_gate = g_gate[:, :half_width] + sent[0]
    grad_up = g_up[:, :half_width] + sent[1]
    grad_down = g_down[:half_width] + sent[2]
    return (
        input_grad,
        grad_gate.astype(jnp.bfloat16)[None],
        grad_up.astype(jnp.bfloat16)[None],
        grad_down.astype(jnp.bfloat16)[None],
    )


MESH = pl.DeviceIdType.MESH
F32 = jnp.float32
BF16 = jnp.bfloat16


def dot(left, right, dims=(((1,), (0,)), ((), ()))):
    return lax.dot_general(left, right, dims, preferred_element_type=F32)


def step_kernel(
    slots,
    n_ex,
    cap,
    direct,
    routes_ref,
    probs_ref,
    place_ref,
    xo_hbm,
    xt_hbm,
    w0_ref,
    w1_ref,
    w2_ref,
    w3_ref,
    w4_ref,
    w5_ref,
    ig_hbm,
    gg_hbm,
    gu_hbm,
    gd_hbm,
    xo_ref,
    xt_ref,
    ig_ref,
    gg_ref,
    gu_ref,
    gd_ref,
    io_sem,
    wg,
    wu,
    wd,
    sx,
    rx,
    pd,
    pr,
    ret,
    rc,
    pre_g,
    pre_u,
    hid,
    dgu,
    meta,
    raw,
    part_out,
    part_in,
    puts,
    takes,
    sy,
    rety,
    rawy,
    party_out,
    party_in,
    w_sem,
    meta_sem,
    raw_sem,
    part_sem,
    out_send,
    out_recv,
    fwd_send,
    fwd_recv,
    pair_send,
    pair_recv,
    back_send,
    back_recv,
    side_sem,
    outy_send,
    outy_recv,
    backy_send,
    backy_recv,
):
    tok, width = xo_ref.shape
    near = slots // 2
    half_rows = near * cap
    dp, ex = lax.axis_index("dp"), lax.axis_index("expert")
    side = lax.rem(ex, 2)
    planes = n_ex // 2
    group = slots // planes
    z = lax.div(ex, 2)
    z_far = lax.rem(z + planes // 2, planes)
    me = dp * planes + z
    me_far = dp * planes + z_far
    partner = (dp, 2 * z + 1 - side)
    twin = (dp, 2 * z_far + side)
    cross = (dp, 2 * z_far + 1 - side)

    middle = direct + (width - direct) // 512 * 256
    spans = ([(0, direct)] if direct else []) + [(direct, middle), (middle, width)]
    paired = [i for i, span in enumerate(spans) if span[0] >= direct]
    n_span = len(spans)
    first, second = paired

    def other(i):
        mask = lax.rem(i, group) * planes + lax.div(i, group)
        slot, power = 0, 1
        while power < slots:
            bit = lax.rem(lax.rem(lax.div(me, power), 2) + lax.rem(lax.div(mask, power), 2), 2)
            slot, power = slot + bit * power, 2 * power
        return slot

    def peer(o):
        unit = 2 * other(lax.rem(o, near)) + side
        return (lax.div(unit, n_ex), lax.rem(unit, n_ex))

    def chunk(index, many=1):
        return pl.ds(pl.multiple_of(index * cap, cap), many * cap)

    def each(low, high, body):
        def step(o, carry):
            body(o)
            return carry

        lax.fori_loop(low, high, step, 0)

    def each_down(low, high, body):
        each(0, high - low, lambda o: body(high - 1 - o))

    def columns(body, low=0, high=width, tile=256):
        each(
            low // tile, high // tile, lambda i: body(pl.ds(pl.multiple_of(i * tile, tile), tile))
        )

    def strips(body, low=0, high=width, tile=512):
        for start in range(low, high, tile):
            body(pl.ds(start, min(tile, high - start)))

    def remote(source, target, send, recv, device):
        return pltpu.make_async_remote_copy(
            src_ref=source,
            dst_ref=target,
            send_sem=send,
            recv_sem=recv,
            device_id=device,
            device_id_type=MESH,
        )

    input_copies = [
        pltpu.make_async_copy(xo_hbm, xo_ref, io_sem.at[0]),
        pltpu.make_async_copy(xt_hbm, xt_ref, io_sem.at[1]),
    ]
    for copy in input_copies:
        copy.start()

    barrier = pltpu.get_barrier_semaphore()
    each(
        1,
        near,
        lambda o: pl.semaphore_signal(barrier, inc=1, device_id=peer(o), device_id_type=MESH),
    )
    for device in (partner, twin, cross):
        pl.semaphore_signal(barrier, inc=1, device_id=device, device_id_type=MESH)

    weight_copies = [
        pltpu.make_async_copy(source, target, w_sem.at[i])
        for i, (source, target) in enumerate(
            [
                (w0_ref, wg.at[0]),
                (w1_ref, wu.at[0]),
                (w2_ref, wd.at[0]),
                (w3_ref, wg.at[1]),
                (w4_ref, wu.at[1]),
                (w5_ref, wd.at[1]),
            ]
        )
    ]
    for copy in weight_copies:
        copy.start()

    def one_hot(compare):
        return jnp.where(compare, 1.0, 0.0).astype(BF16)

    def stand(line):
        size = line.shape[1]
        here = [lax.broadcasted_iota(jnp.int32, (size, size), d) for d in range(2)]
        return jnp.sum(jnp.where(here[0] == here[1], line, 0.0), axis=1, keepdims=True)

    def count(mask, axis):
        return jnp.sum(jnp.where(mask, 1.0, 0.0), axis=axis, keepdims=True)

    meta[0, 0:2, :] = routes_ref[...].astype(F32)
    meta[0, 2:4, :] = probs_ref[...]
    meta[0, 4:8, :] = jnp.zeros((4, tok), F32)

    def meta_copy(block):
        device = (twin, partner, cross)[block - 1]
        sem = meta_sem.at[0, block - 1], meta_sem.at[1, block - 1]
        return remote(meta.at[0], meta.at[block], *sem, device)

    def order_of(slot, home):
        mask = slot.astype(jnp.int32) ^ home
        return lax.rem(mask, planes) * group + lax.div(mask, planes)

    def tables(block):
        home = me_far if block % 2 else me
        low = half_rows * (block % 2)
        down, across = [lax.broadcasted_iota(jnp.int32, (tok, tok), d) for d in range(2)]
        line = [meta[block, k : k + 1, :] for k in range(2)]
        tall = [stand(line[k]) for k in range(2)]
        place = place_ref[...].astype(F32)
        place_tall = stand(place)
        ids_line = lax.broadcasted_iota(jnp.int32, (tok, slots), 1).astype(F32)
        ids_tall = lax.broadcasted_iota(jnp.int32, (slots, tok), 0).astype(F32)
        row_iota = lax.broadcasted_iota(jnp.int32, (half_rows, tok), 0) + low
        col_iota = lax.broadcasted_iota(jnp.int32, (tok, half_rows), 1) + low
        for k in range(2):
            alike = (line[k] == tall[0]) | (line[k] == tall[1])
            slot = jnp.sum(jnp.where(ids_tall == line[k], place_tall, 0.0), axis=0, keepdims=True)
            before = count(alike & (down < across), 0).astype(jnp.int32)
            puts[block, k] = one_hot(row_iota == order_of(slot, home) * cap + before)
            alike = (tall[k] == line[0]) | (tall[k] == line[1])
            slot = jnp.sum(jnp.where(ids_line == tall[k], place, 0.0), axis=1, keepdims=True)
            before = count(alike & (across < down), 1).astype(jnp.int32)
            takes[block, k] = one_hot(col_iota == order_of(slot, home) * cap + before)

    def probs_of(block):
        return [stand(meta[block, 2 + k : 3 + k, :]) for k in range(2)]

    def rows_of(block):
        return pl.ds(half_rows * (block % 2), half_rows)

    def place_rows(target, block, source, low, high):
        put = puts[block, 0] + puts[block, 1]

        def body(cols):
            target[rows_of(block), cols] = dot(put, source[:, cols]).astype(BF16)

        strips(body, low, high)

    def span_of(step):
        return (0, width) if step < 2 else spans[step - 2]

    def into(step):
        return rx.at[step] if step < 2 else rc

    def out_copy(step, o, many=1):
        low, high = span_of(step)
        cols = pl.ds(low, high - low)
        return remote(
            sx.at[min(step, 2), chunk(o, many), cols],
            into(step).at[0, chunk(o, many), cols],
            out_send.at[step, lax.div(o, near)],
            out_recv.at[step, o],
            peer(o),
        )

    def fwd_copy(step, o, many=1):
        low, high = span_of(step)
        low = max(low, direct)
        here = into(step)
        cols = pl.ds(low, high - low)
        return remote(
            here.at[0, chunk(o, many), cols],
            here.at[1, chunk(o, many), cols],
            fwd_send.at[step, lax.div(o, near)],
            fwd_recv.at[step, lax.div(o, near)],
            partner,
        )

    forwarded = [0, 1] + [2 + i for i in paired]

    def begin(step, block):
        base = near * block
        each(base + 1, base + near, lambda o: out_copy(step, o).start())
        low, high = span_of(step)
        cols = pl.ds(low, high - low)
        into(step)[0, pl.ds(base * cap, cap), cols] = sx[min(step, 2), pl.ds(base * cap, cap), cols]
        if step in forwarded:
            fwd_copy(step, base).start()

    def relay(step, low, high):
        def body(o):
            out_copy(step, o).wait_recv()
            if step in forwarded:
                fwd_copy(step, o).start()

        each(low, high, body)

    def arrived(step, block):
        fwd_copy(step, near * block, near).wait_recv()

    def outy_copy(step, o, many=1):
        target = rx.at[step] if step < 2 else rc
        return remote(
            sy.at[step, chunk(o, many)],
            target.at[1, chunk(o, many), pl.ds(0, direct)],
            outy_send.at[step, lax.div(o, near)],
            outy_recv.at[step, lax.div(o, near)],
            peer(o),
        )

    def beginy(step, block):
        base = near * block
        each(base + 1, base + near, lambda o: outy_copy(step, o).start())
        target = rx.at[step] if step < 2 else rc
        target[1, pl.ds(base * cap, cap), 0:direct] = sy[step, pl.ds(base * cap, cap)]

    def arrivedy(step, block):
        outy_copy(step, near * block + 1, near - 1).wait_recv()

    def raw_copy(step):
        low, high = span_of(step)
        cols = pl.ds(low, high - low)
        source = (xo_ref, xt_ref)[step] if step < 2 else part_out.at[2]
        return remote(
            source.at[:, cols],
            raw.at[min(step, 2), :, cols],
            raw_sem.at[0, step],
            raw_sem.at[1, step],
            twin,
        )

    def side_copy(step, block):
        cols = pl.ds(0, direct)
        source = (xo_ref, xt_ref, part_out.at[2])[step] if block == 0 else raw.at[step]
        return remote(
            source.at[:, cols],
            rawy.at[step, block],
            side_sem.at[0, 2 * step + block],
            side_sem.at[1, 2 * step + block],
            partner,
        )

    def half_cols(turn):
        low, high = spans[turn % n_span]
        return pl.ds(low, high - low)

    def paired_turn(turn):
        return 2 * (turn // n_span) + paired.index(turn % n_span)

    def pair_copy(turn, o, many=1):
        return remote(
            pd.at[1, chunk(o, many), half_cols(turn)],
            pr.at[turn // n_span, chunk(o, many), half_cols(turn)],
            pair_send.at[paired_turn(turn), lax.div(o, near)],
            pair_recv.at[paired_turn(turn), o],
            partner,
        )

    def back_copy(turn, o, many=1):
        return remote(
            pd.at[0, chunk(o, many), half_cols(turn)],
            ret.at[turn // n_span, chunk(o, many), half_cols(turn)],
            back_send.at[turn, lax.div(o, near)],
            back_recv.at[turn, lax.div(o, near)],
            peer(o),
        )

    def backy_copy(way, o, many=1):
        return remote(
            pd.at[1, chunk(o, many), pl.ds(0, direct)],
            rety.at[way, chunk(o, many)],
            backy_send.at[way, lax.div(o, near)],
            backy_recv.at[way, lax.div(o, near)],
            peer(o),
        )

    def add_part(turn, o):
        pair_copy(turn, o).wait_recv()
        cols = half_cols(turn)
        total = pd[0, chunk(o), cols].astype(F32) + pr[turn // n_span, chunk(o), cols].astype(F32)
        return total.astype(BF16)

    def give_back(turn, block):
        base = near * block

        def body(o):
            pd[0, chunk(o), half_cols(turn)] = add_part(turn, o)
            back_copy(turn, o).start()

        each_down(base + 1, base + near, body)
        ret[turn // n_span, pl.ds(base * cap, cap), half_cols(turn)] = add_part(turn, base)

    def give_direct(way, block):
        base, turn = near * block, n_span * way

        def body(o):
            back_copy(turn, o).start()
            backy_copy(way, o).start()

        each_down(base + 1, base + near, body)
        own = pl.ds(base * cap, cap)
        ret[way, own, 0:direct] = pd[0, own, 0:direct]
        rety[way, own] = pd[1, own, 0:direct]

    def back_came(turn, block):
        back_copy(turn, near * block + 1, near - 1).wait_recv()

    def backy_came(way, block):
        backy_copy(way, near * block + 1, near - 1).wait_recv()

    def part_copy(turn):
        way, cols = turn // n_span, half_cols(turn)
        return remote(
            part_out.at[way, :, cols],
            part_in.at[way, :, cols],
            part_sem.at[0, turn],
            part_sem.at[1, turn],
            twin,
        )

    def party_copy(way, block):
        return remote(
            party_out.at[way, block],
            party_in.at[way, block],
            side_sem.at[0, 6 + 2 * way + block],
            side_sem.at[1, 6 + 2 * way + block],
            partner,
        )

    def picked(way, block, source):
        if way == 0:
            p0, p1 = probs_of(block)
            return p0 * dot(takes[block, 0], source) + p1 * dot(takes[block, 1], source)
        return dot(takes[block, 0] + takes[block, 1], source)

    def send_side(way, block):
        backy_came(way, block)
        rows = rows_of(block)

        def body(cols):
            party_out[way, block, :, cols] = picked(way, 2 + block, rety[way, rows, cols]).astype(
                BF16
            )

        strips(body, 0, direct)
        party_copy(way, block).start()

    def send_part(turn):
        way = turn // n_span
        straight = spans[turn % n_span][0] < direct
        back_came(turn, 1)
        if straight:
            party_copy(way, 1).wait_recv()

        def body(cols):
            total = picked(way, 1, ret[way, rows_of(1), cols])
            if straight:
                total = total + party_in[way, 1, :, cols].astype(F32)
            part_out[way, :, cols] = total.astype(BF16)

        strips(body, *spans[turn % n_span])
        part_copy(turn).start()

    def whole(turn, use):
        way = turn // n_span
        straight = spans[turn % n_span][0] < direct
        back_came(turn, 0)
        if straight:
            party_copy(way, 0).wait_recv()
        part_copy(turn).wait_recv()

        def body(cols):
            total = picked(way, 0, ret[way, rows_of(0), cols])
            total = total + part_in[way, :, cols].astype(F32)
            if straight:
                total = total + party_in[way, 0, :, cols].astype(F32)
            use(cols, total)

        strips(body, *spans[turn % n_span])

    def cotangents(block, diff):
        p0, p1 = probs_of(block)
        rows0, rows1 = (p0 * diff).astype(BF16), (p1 * diff).astype(BF16)
        return (dot(puts[block, 0], rows0) + dot(puts[block, 1], rows1)).astype(BF16)

    def own_cotangents(index):
        def use(cols, diff):
            part_out[2, :, cols] = diff.astype(BF16)
            sx[2, rows_of(0), cols] = cotangents(0, diff)

        whole(index, use)
        raw_copy(2 + index).start()
        if spans[index][0] < direct:
            side_copy(2, 0).start()
        begin(2 + index, 0)

    def twin_cotangents(index):
        raw_copy(2 + index).wait_recv()
        if spans[index][0] < direct:
            side_copy(2, 1).start()

        def body(cols):
            sx[2, rows_of(1), cols] = cotangents(1, raw[2, :, cols].astype(F32))

        strips(body, *spans[index])
        begin(2 + index, 1)

    def side_cotangents(block):
        side_copy(2, block).wait_recv()

        def body(cols):
            sy[2, rows_of(block), cols] = cotangents(2 + block, rawy[2, block, :, cols].astype(F32))

        strips(body, 0, direct)
        beginy(2, block)

    def side_inputs(net, block):
        side_copy(net, block).wait_recv()
        place_rows(sy.at[net], 2 + block, rawy.at[net, block], 0, direct)
        beginy(net, block)

    def forward(net, part, block):
        rows = rows_of(block)
        gate = dot(rx[net, part, rows], wg[net])
        up = dot(rx[net, part, rows], wu[net])
        hid[net, part, rows] = (gate * jax.nn.sigmoid(gate) * up).astype(BF16)
        if net == 0:
            pre_g[part, rows] = gate
            pre_u[part, rows] = up

    tables(0)
    input_copies[0].wait()
    place_rows(sx.at[0], 0, xo_ref, 0, width)
    pl.semaphore_wait(barrier, near + 2)
    for block in (1, 2, 3):
        meta_copy(block).start()
    raw_copy(0).start()
    begin(0, 0)
    if direct:
        side_copy(0, 0).start()
    input_copies[1].wait()
    place_rows(sx.at[1], 0, xt_ref, 0, width)
    begin(1, 0)
    if direct:
        side_copy(1, 0).start()
    relay(0, 1, near // 2)
    for block in (2, 1, 3):
        meta_copy(block).wait_recv()
    if direct:
        tables(2)
        side_inputs(0, 0)
    relay(0, near // 2, near)
    tables(1)
    if direct:
        side_inputs(1, 0)
    relay(1, 1, near // 2)
    raw_copy(0).wait_recv()
    raw_copy(0).wait_send()
    raw_copy(1).start()
    place_rows(sx.at[0], 1, raw.at[0], 0, width)
    begin(0, 1)
    if direct:
        side_copy(0, 1).start()
        tables(3)
    relay(1, near // 2, near)
    for copy in weight_copies:
        copy.wait()
    forward(0, 0, 0)
    relay(0, near + 1, slots)
    if direct:
        side_inputs(0, 1)
    raw_copy(1).wait_recv()
    place_rows(sx.at[1], 1, raw.at[1], 0, width)
    begin(1, 1)
    if direct:
        side_copy(1, 1).start()

    def landed(step, block):
        arrived(step, block)
        if direct and step < 2:
            arrivedy(step, block)

    forward(1, 0, 0)
    forward(0, 0, 1)
    landed(0, 0)
    forward(0, 1, 0)
    relay(1, near + 1, slots)
    if direct:
        side_inputs(1, 1)
    forward(1, 0, 1)
    landed(0, 1)
    forward(0, 1, 1)

    def outputs(index, part, block):
        rows = rows_of(block)

        def body(cols):
            diff = dot(hid[0, part, rows], wd[0, :, cols]) - dot(hid[1, part, rows], wd[1, :, cols])
            pd[part, rows, cols] = diff.astype(BF16)

        strips(body, *spans[index])

    def row_grads(index, part, block):
        rows = rows_of(block)

        def body(cols):
            total = dot(dgu[0, part, rows], wg[0, cols, :], contract_last)
            total = total + dot(dgu[1, part, rows], wu[0, cols, :], contract_last)
            pd[part, rows, cols] = total.astype(BF16)

        strips(body, *spans[index])

    def exchange(rows_out, way, block, index):
        rows_out(index, 1, block)
        turn = n_span * way + index
        each_down(near * block, near * block + near, lambda o: pair_copy(turn, o).start())

    def way_back(rows_out, way, ready):
        for block in (0, 1):
            ready(block)
            if direct:
                for part in (0, 1):
                    rows_out(0, part, block)
                give_direct(way, block)
            exchange(rows_out, way, block, first)
        for block in (0, 1):
            rows_out(first, 0, block)
        if direct:
            send_side(way, 1)
            send_side(way, 0)
        for block in (1, 0):
            exchange(rows_out, way, block, second)
        for block in (1, 0):
            rows_out(second, 0, block)

    def ready_outputs(block):
        landed(1, block)
        forward(1, 1, block)

    way_back(outputs, 0, ready_outputs)
    give_back(first, 0)
    give_back(first, 1)
    if direct:
        send_part(0)
    send_part(first)
    if direct:
        own_cotangents(0)
    give_back(second, 1)
    own_cotangents(first)
    if direct:
        twin_cotangents(0)
    send_part(second)
    give_back(second, 0)
    relay(2 + first, 1, near)
    twin_cotangents(first)
    own_cotangents(second)
    if direct:
        side_cotangents(0)
    relay(2 + first, near + 1, slots)
    relay(2 + second, 1, near)
    if direct:
        side_cotangents(1)
    twin_cotangents(second)
    relay(2 + second, near + 1, slots)
    if direct:
        relay(2, 1, near)
        relay(2, near + 1, slots)

    def hidden_back(part, block):
        rows = rows_of(block)
        d_hidden = dot(rc[part, rows], wd[0], contract_last)
        gate, up = pre_g[part, rows], pre_u[part, rows]
        sig = jax.nn.sigmoid(gate)
        dgu[0, part, rows] = (d_hidden * up * sig * (1.0 + gate * (1.0 - sig))).astype(BF16)
        dgu[1, part, rows] = (d_hidden * (gate * sig)).astype(BF16)

    def went(way):
        for base in (0, near):
            for index in paired:
                pair_copy(n_span * way + index, base, near).wait_send()
            for index in range(n_span):
                back_copy(n_span * way + index, base + 1, near - 1).wait_send()
            if direct:
                backy_copy(way, base + 1, near - 1).wait_send()

    went(0)
    hidden_back(0, 0)
    hidden_back(0, 1)

    def ready_grads(block):
        if direct:
            arrivedy(2, block)
        for index in paired:
            arrived(2 + index, block)
        hidden_back(1, block)

    way_back(row_grads, 1, ready_grads)

    def weight_grads(cols):
        for index, target in ((0, gg_ref), (1, gu_ref)):
            total = dot(rx[0, 0, :, cols], dgu[index, 0], contract_first)
            total = total + dot(rx[0, 1, :, cols], dgu[index, 1], contract_first)
            target[cols, :] = total.astype(BF16)
        total = dot(hid[0, 0], rc[0, :, cols], contract_first)
        total = total + dot(hid[0, 1], rc[1, :, cols], contract_first)
        gd_ref[:, cols] = total.astype(BF16)

    def inputs_grad(cols, total):
        ig_ref[:, cols] = total.astype(BF16)

    strips(weight_grads, 0, width)
    weight_grad_copies = [
        pltpu.make_async_copy(source, target, io_sem.at[2 + i])
        for i, (source, target) in enumerate(
            [(gg_ref, gg_hbm), (gu_ref, gu_hbm), (gd_ref, gd_hbm)]
        )
    ]
    for copy in weight_grad_copies:
        copy.start()

    def grad_copy(index):
        cols = half_cols(index)
        return pltpu.make_async_copy(ig_ref.at[:, cols], ig_hbm.at[:, cols], io_sem.at[5 + index])

    give_back(n_span + first, 0)
    give_back(n_span + first, 1)
    if direct:
        send_part(n_span)
    send_part(n_span + first)
    if direct:
        whole(n_span, inputs_grad)
        grad_copy(0).start()
    give_back(n_span + second, 1)
    send_part(n_span + second)
    whole(n_span + first, inputs_grad)
    grad_copy(first).start()
    give_back(n_span + second, 0)

    for step in range(2 + n_span):
        if step != 0:
            raw_copy(step).wait_send()
        for base in (0, near):
            out_copy(step, base + 1, near - 1).wait_send()
            if step in forwarded:
                fwd_copy(step, base, near).wait_send()
    for block in (1, 2, 3):
        meta_copy(block).wait_send()
    for turn in range(2 * n_span):
        part_copy(turn).wait_send()
    if direct:
        for step in range(3):
            for block in (0, 1):
                side_copy(step, block).wait_send()
                outy_copy(step, near * block + 1, near - 1).wait_send()
        for way in (0, 1):
            for block in (0, 1):
                party_copy(way, block).wait_send()
    whole(n_span + second, inputs_grad)
    grad_copy(second).start()
    went(1)
    for index in range(n_span):
        grad_copy(index).wait()
    for copy in weight_grad_copies:
        copy.wait()


def hand_over(pieces, *refs):
    come, leave = refs[12], refs[13]
    given, taken = [], []
    for i in range(4):
        size = refs[i].shape[0] // pieces
        for piece in range(pieces):
            rows = pl.ds(piece * size, size)
            held = refs[8 + i].at[rows]
            given.append(pltpu.make_async_copy(refs[i].at[rows], held, come.at[i, piece]))
            taken.append(pltpu.make_async_copy(held, refs[4 + i].at[rows], leave.at[i, piece]))
    for copy in given:
        copy.start()
    for copy, later in zip(given, taken):
        copy.wait()
        later.start()
    for copy in taken:
        copy.wait()


def shards(
    x_online,
    x_target,
    routes,
    gate_probs,
    expert_place,
    gate_online,
    up_online,
    down_online,
    gate_target,
    up_target,
    down_target,
):
    tok, width = x_online.shape
    slots = expert_place.shape[0]
    n_ex = lax.axis_size("expert")
    cap = 2 * ((2 * tok + slots - 1) // slots)
    rows = slots * cap
    half = gate_online.shape[2]
    paired = 2 * slots == lax.axis_size("dp") * n_ex and n_ex % 2 == 0
    halving = slots & (slots - 1) == 0 and n_ex & (n_ex - 1) == 0
    if cap % 16 or width % 1024 or tok % 128 or slots < 16 or n_ex < 4 or not (paired and halving):
        return shards_plain(
            x_online,
            x_target,
            routes,
            gate_probs,
            expert_place,
            gate_online,
            up_online,
            down_online,
            gate_target,
            up_target,
            down_target,
        )
    direct = 256
    n_span = 3 if direct else 2
    side_cols = max(direct, 128)
    near = slots // 2
    vmem = pl.BlockSpec(memory_space=pltpu.VMEM)
    hbm = pl.BlockSpec(memory_space=pl.ANY)
    dma = pltpu.SemaphoreType.DMA
    outs = pl.pallas_call(
        functools.partial(step_kernel, slots, n_ex, cap, direct),
        out_shape=(
            jax.ShapeDtypeStruct((tok, width), BF16),
            jax.ShapeDtypeStruct((width, half), BF16),
            jax.ShapeDtypeStruct((width, half), BF16),
            jax.ShapeDtypeStruct((half, width), BF16),
        ),
        in_specs=[vmem] * 3 + [hbm] * 8,
        out_specs=(hbm,) * 4,
        scratch_shapes=[
            pltpu.VMEM((tok, width), BF16),
            pltpu.VMEM((tok, width), BF16),
            pltpu.VMEM((tok, width), BF16),
            pltpu.VMEM((width, half), BF16),
            pltpu.VMEM((width, half), BF16),
            pltpu.VMEM((half, width), BF16),
            dma((8,)),
            pltpu.VMEM((2, width, half), BF16),
            pltpu.VMEM((2, width, half), BF16),
            pltpu.VMEM((2, half, width), BF16),
            pltpu.VMEM((3, rows, width), BF16),
            pltpu.VMEM((2, 2, rows, width), BF16),
            pltpu.VMEM((2, rows, width), BF16),
            pltpu.VMEM((2, rows, width), BF16),
            pltpu.VMEM((2, rows, width), BF16),
            pltpu.VMEM((2, rows, width), BF16),
            pltpu.VMEM((2, rows, half), F32),
            pltpu.VMEM((2, rows, half), F32),
            pltpu.VMEM((2, 2, rows, half), BF16),
            pltpu.VMEM((2, 2, rows, half), BF16),
            pltpu.VMEM((4, 8, tok), F32),
            pltpu.VMEM((3, tok, width), BF16),
            pltpu.VMEM((3, tok, width), BF16),
            pltpu.VMEM((2, tok, width), BF16),
            pltpu.VMEM((4, 2, near * cap, tok), BF16),
            pltpu.VMEM((4, 2, tok, near * cap), BF16),
            pltpu.VMEM((3, rows, side_cols), BF16),
            pltpu.VMEM((2, rows, side_cols), BF16),
            pltpu.VMEM((3, 2, tok, side_cols), BF16),
            pltpu.VMEM((2, 2, tok, side_cols), BF16),
            pltpu.VMEM((2, 2, tok, side_cols), BF16),
            dma((6,)),
            dma((2, 3)),
            dma((2, 2 + n_span)),
            dma((2, 2 * n_span)),
            dma((2 + n_span, 2)),
            dma((2 + n_span, slots)),
            dma((2 + n_span, 2)),
            dma((2 + n_span, 2)),
            dma((4, 2)),
            dma((4, slots)),
            dma((2 * n_span, 2)),
            dma((2 * n_span, 2)),
            dma((2, 10)),
            dma((3, 2)),
            dma((3, 2)),
            dma((2, 2)),
            dma((2, 2)),
        ],
        compiler_params=pltpu.CompilerParams(
            collective_id=0, has_side_effects=True, vmem_limit_bytes=60 * 2**20
        ),
    )(
        routes.T,
        gate_probs.T,
        expert_place[None],
        x_online,
        x_target,
        gate_online[0],
        up_online[0],
        down_online[0],
        gate_target[0],
        up_target[0],
        down_target[0],
    )
    pieces = 1
    outs = pl.pallas_call(
        functools.partial(hand_over, pieces),
        out_shape=tuple(jax.ShapeDtypeStruct(o.shape, o.dtype) for o in outs),
        in_specs=[hbm] * 4,
        out_specs=(hbm,) * 4,
        scratch_shapes=[pltpu.VMEM(o.shape, o.dtype) for o in outs]
        + [dma((4, pieces)), dma((4, pieces))],
    )(*outs)
    return (outs[0], outs[1][None], outs[2][None], outs[3][None])


def solution(mesh):
    in_specs = (
        P(("dp", "expert"), None),
        P(("dp", "expert"), None),
        P(("dp", "expert"), None),
        P(("dp", "expert"), None),
        P(),
        P(("dp", "expert"), None, None),
        P(("dp", "expert"), None, None),
        P(("dp", "expert"), None, None),
        P(("dp", "expert"), None, None),
        P(("dp", "expert"), None, None),
        P(("dp", "expert"), None, None),
    )
    out_specs = (
        P(("dp", "expert"), None),
        P(("dp", "expert"), None, None),
        P(("dp", "expert"), None, None),
        P(("dp", "expert"), None, None),
    )
    return jax.shard_map(shards, mesh=mesh, in_specs=in_specs, out_specs=out_specs, check_vma=False)
```
